128 devices in a mesh: gx: 16 (over z, y), gy: 8 (over x, core).
Axes of the slice: x: 4, y: 4, z: 4, core: 2. Of those that a mesh axis runs over, the one named last changes fastest.
Arguments:
- features: bfloat16 [262144, 512], P(('gx', 'gy')), may hold values from -6 to 6
- point_block: int32 [262144], P(('gx', 'gy')), may hold values from 0 to 15, as said below
- block_count: int32 [128], P(('gx', 'gy')), may hold values from 1 to 16, as said below
- z_dest_dev: int32 [128, 16], P(('gx', 'gy')), may hold values from 0 to 15, as said below
- z_dest_slot: int32 [128, 16], P(('gx', 'gy')), may hold values from 0 to 7
- z_back_owner: int32 [128, 8], P(('gx', 'gy')), may hold values from 0 to 15, as said below
- z_back_block: int32 [128, 8], P(('gx', 'gy')), may hold values from 0 to 15, as said below
- hil_dest_dev: int32 [128, 8], P(('gx', 'gy')), may hold values from 0 to 7, as said below
- hil_dest_slot: int32 [128, 8], P(('gx', 'gy')), may hold values from 0 to 7
- hil_back_dev: int32 [128, 8], P(('gx', 'gy')), may hold values from 0 to 7, as said below
- hil_back_slot: int32 [128, 8], P(('gx', 'gy')), may hold values from 0 to 7, as said below
- norm_gain: float32 [2, 2, 512], replicated, may hold values from 0.5 to 1.5
- w_qkv: bfloat16 [2, 512, 1536], replicated
- w_out: bfloat16 [2, 512, 512], replicated, may hold values from -0.25 to 0.25
- w_up: bfloat16 [2, 512, 2048], replicated, may hold values from -0.25 to 0.25
- w_down: bfloat16 [2, 2048, 512], replicated, may hold values from -0.125 to 0.125
Outputs:
- returned: bfloat16 [262144, 512], P(('gx', 'gy'))
The draws below stay inside these ranges and needn't reach their ends.
Inputs may be any that keep to these rules, and one draw needn't show every extreme that they name: `point_block`: on each owner every id below its block_count names exactly 128 rows; rows with ids at or above it are dead. `block_count`: along each gx line of owners (one gy index) the counts sum to 128, and some owner of every line holds 16 blocks. `z_dest_dev`: along each gx line the live blocks fill every (device, slot) exactly once; at most 1 live blocks of one owner go to one device, a bound reached in every line; entries of dead blocks are arbitrary. `z_back_owner`: the inverse of z_dest_dev and z_dest_slot on live blocks. `z_back_block`: the inverse of z_dest_dev and z_dest_slot on live blocks. `hil_dest_dev`: along each gy line the slots are permuted among devices; every device sends exactly 2 blocks to each device it sends to. `hil_back_dev`: the inverse of hil_dest_dev and hil_dest_slot. `hil_back_slot`: the inverse of hil_dest_dev and hil_dest_slot.
All inputs are finite; a program needn't handle non-finite values.
Results may differ from the reference program's by a relative error of at most 0.023.
The reference program's roundings to bfloat16 on the way count: a program that leaves them out, or rounds other values in their place, can miss the bound.
Values may be sent and summed in bfloat16 or wider, within the bound.
A program may use at most 128 MiB of HBM per device.

```python
import jax
import jax.numpy as jnp
from jax import lax

D = 512
HEADS = 8
FF = 2048
PATCH = 1024
BLOCK = 128
LAYERS = 2
PATCHES_DEV = 1
BLOCKS_DEV = 8
CAP = 16
ROWS = 2048
HPAIR = 2
N_GX = 16
N_GY = 8
DEVICES = 128


def line_plan(key):
    subkeys = jax.random.split(key, 6)
    crowded = jax.random.randint(subkeys[0], (), 0, N_GX)
    headroom = CAP - 1
    spare_count = N_GX * BLOCKS_DEV - CAP - (N_GX - 1)
    cell_order = jax.random.permutation(subkeys[1], (N_GX - 1) * headroom)
    chosen = jnp.arange((N_GX - 1) * headroom) < spare_count
    holder = cell_order // headroom
    extras = jnp.sum(((holder[None, :] == jnp.arange(N_GX - 1)[:, None]) & chosen[None, :]).astype(jnp.int32), axis=1)
    owners = jnp.arange(N_GX, dtype=jnp.int32)
    others = jnp.clip(owners - (owners > crowded).astype(jnp.int32), 0, N_GX - 2)
    counts = jnp.where(owners == crowded, CAP, 1 + extras[others]).astype(jnp.int32)
    starts = jnp.cumsum(counts) - counts
    block_ids = jnp.arange(CAP, dtype=jnp.int32)
    alive = block_ids[None, :] < counts[:, None]
    scores = jax.random.randint(subkeys[2], (N_GX, CAP), 0, 1 << 20)
    sort_key = jnp.where(alive, scores, 1 << 20) * CAP + block_ids[None, :]
    ranking = jnp.argsort(jnp.argsort(sort_key, axis=1), axis=1).astype(jnp.int32)
    order_index = starts[:, None] + ranking
    rotate = jax.random.randint(subkeys[3], (), 0, N_GX)
    target = (order_index + rotate) % N_GX
    target_slot = order_index // N_GX
    junk_dest = jax.random.randint(subkeys[4], (N_GX, CAP), 0, N_GX)
    junk_slot = jax.random.randint(subkeys[5], (N_GX, CAP), 0, BLOCKS_DEV)
    dest_all = jnp.where(alive, target, junk_dest).astype(jnp.int32)
    slot_all = jnp.where(alive, target_slot, junk_slot).astype(jnp.int32)
    flat_index = jnp.where(alive, target * BLOCKS_DEV + target_slot, N_GX * BLOCKS_DEV).reshape(-1)
    owner_grid = jnp.broadcast_to(owners[:, None], (N_GX, CAP)).reshape(-1)
    block_grid = jnp.broadcast_to(block_ids[None, :], (N_GX, CAP)).reshape(-1)
    back_owner = jnp.zeros(N_GX * BLOCKS_DEV, jnp.int32).at[flat_index].set(owner_grid, mode='drop')
    back_block = jnp.zeros(N_GX * BLOCKS_DEV, jnp.int32).at[flat_index].set(block_grid, mode='drop')
    return (counts, dest_all, slot_all, back_owner.reshape(N_GX, BLOCKS_DEV), back_block.reshape(N_GX, BLOCKS_DEV))


def z_plan(key):
    planned = jax.vmap(line_plan)(jax.random.split(jax.random.fold_in(key, 71), N_GY))

    def layout(grid):
        return jnp.swapaxes(grid, 0, 1).reshape((N_GX * N_GY,) + grid.shape[2:])
    return tuple((layout(grid) for grid in planned))


def column_plan(key):
    subkeys = jax.random.split(key, 3)
    offsets = jax.random.permutation(subkeys[0], N_GY)[:4]
    source_perm = jax.vmap(lambda k: jax.random.permutation(k, BLOCKS_DEV))(jax.random.split(subkeys[1], N_GY)).astype(jnp.int32)
    arrival_perm = jax.vmap(lambda k: jax.random.permutation(k, BLOCKS_DEV))(jax.random.split(subkeys[2], N_GY)).astype(jnp.int32)
    members = jnp.arange(BLOCKS_DEV, dtype=jnp.int32)
    sources = jnp.arange(N_GY, dtype=jnp.int32)
    dest_by_member = ((sources[:, None] + offsets[members // HPAIR][None, :]) % N_GY).astype(jnp.int32)
    slot_by_member = arrival_perm[dest_by_member, jnp.broadcast_to(members[None, :], (N_GY, BLOCKS_DEV))]
    source_grid = jnp.broadcast_to(sources[:, None], (N_GY, BLOCKS_DEV))
    dest_dev = jnp.zeros((N_GY, BLOCKS_DEV), jnp.int32).at[source_grid, source_perm].set(dest_by_member)
    dest_slot = jnp.zeros((N_GY, BLOCKS_DEV), jnp.int32).at[source_grid, source_perm].set(slot_by_member)
    back_dev = jnp.zeros((N_GY, BLOCKS_DEV), jnp.int32).at[dest_by_member, slot_by_member].set(source_grid)
    back_slot = jnp.zeros((N_GY, BLOCKS_DEV), jnp.int32).at[dest_by_member, slot_by_member].set(source_perm)
    return (dest_dev, dest_slot, back_dev, back_slot)


def h_plan(key):
    planned = jax.vmap(column_plan)(jax.random.split(jax.random.fold_in(key, 83), N_GX))
    return tuple((grid.reshape(N_GX * N_GY, BLOCKS_DEV) for grid in planned))


def draw_point_block(key, part):
    subkeys = jax.random.split(jax.random.fold_in(key, 97), N_GX * N_GY)
    shuffled = jax.vmap(lambda k: jax.random.permutation(k, ROWS))(subkeys)
    return (shuffled // BLOCK).astype(jnp.int32).reshape(-1)


def draw_block_count(key, part):
    return z_plan(key)[0]


def draw_z_dest_dev(key, part):
    return z_plan(key)[1]


def draw_z_dest_slot(key, part):
    return z_plan(key)[2]


def draw_z_back_owner(key, part):
    return z_plan(key)[3]


def draw_z_back_block(key, part):
    return z_plan(key)[4]


def draw_hil_dest_dev(key, part):
    return h_plan(key)[0]


def draw_hil_dest_slot(key, part):
    return h_plan(key)[1]


def draw_hil_back_dev(key, part):
    return h_plan(key)[2]


def draw_hil_back_slot(key, part):
    return h_plan(key)[3]


def draw_w_qkv(key, part):
    weights_raw = jax.random.normal(jax.random.fold_in(key, 5), (LAYERS, D, 3 * D), jnp.float32) * D ** (-0.5)
    return weights_raw.astype(jnp.bfloat16)


def shard_levels(own_key, extent, pieces, least, high):
    factor_of = 1.0
    for dim, blocks in pieces:
        heights = jax.random.uniform(jax.random.fold_in(jax.random.fold_in(own_key, 6), dim), (blocks,), jnp.float32, least / len(pieces), high / len(pieces))
        factor_of = factor_of * jnp.repeat(jnp.exp(heights), extent[dim] // blocks).reshape((-1,) + (1,) * (len(extent) - 1 - dim))
    return factor_of


def bell_draw(rng, shape, width, most, cuts=(), held_as=jnp.bfloat16):
    entries = jax.random.normal(rng, shape, jnp.float32) * width
    if len(cuts) > 0:
        entries = shard_levels(rng, shape, cuts, -0.22, 0.18) * entries
    return jnp.clip(entries, min=-most, max=most).astype(held_as)


def setup_inputs(seed: int = 0) -> dict:
    seeds = jax.random.split(jax.random.key(seed), 17)
    features = bell_draw(seeds[0], (DEVICES * ROWS, D), 1.0, 6.0, ((0, 128),))
    point_block = draw_point_block(jax.random.fold_in(seeds[16], 71), 0)
    block_count = draw_block_count(jax.random.fold_in(seeds[16], 71), 0)
    z_dest_dev = draw_z_dest_dev(jax.random.fold_in(seeds[16], 71), 0)
    z_dest_slot = draw_z_dest_slot(jax.random.fold_in(seeds[16], 71), 0)
    z_back_owner = draw_z_back_owner(jax.random.fold_in(seeds[16], 71), 0)
    z_back_block = draw_z_back_block(jax.random.fold_in(seeds[16], 71), 0)
    hil_dest_dev = draw_hil_dest_dev(jax.random.fold_in(seeds[16], 71), 0)
    hil_dest_slot = draw_hil_dest_slot(jax.random.fold_in(seeds[16], 71), 0)
    hil_back_dev = draw_hil_back_dev(jax.random.fold_in(seeds[16], 71), 0)
    hil_back_slot = draw_hil_back_slot(jax.random.fold_in(seeds[16], 71), 0)
    norm_gain = jnp.clip(1.0 + 0.1 * jax.random.normal(seeds[11], (LAYERS, 2, D), jnp.float32), 0.5, 1.5)
    w_qkv = draw_w_qkv(jax.random.fold_in(seeds[16], 71), 0)
    w_out = bell_draw(seeds[13], (LAYERS, D, D), D ** -0.5, 0.25)
    w_up = bell_draw(seeds[14], (LAYERS, D, FF), D ** -0.5, 0.25)
    w_down = bell_draw(seeds[15], (LAYERS, FF, D), FF ** -0.5, 0.125)
    return dict(features=features, point_block=point_block, block_count=block_count, z_dest_dev=z_dest_dev, z_dest_slot=z_dest_slot, z_back_owner=z_back_owner, z_back_block=z_back_block, hil_dest_dev=hil_dest_dev, hil_dest_slot=hil_dest_slot, hil_back_dev=hil_back_dev, hil_back_slot=hil_back_slot, norm_gain=norm_gain, w_qkv=w_qkv, w_out=w_out, w_up=w_up, w_down=w_down)


EPSILON = 1e-05

def normed(values_in, gain_row):
    centered = values_in - lax.optimization_barrier(jnp.mean(values_in, axis=-1, keepdims=True))
    variance = lax.optimization_barrier(jnp.mean(centered * centered, axis=-1, keepdims=True))
    return centered * lax.rsqrt(variance + EPSILON) * gain_row

def layer_patch(patch_rows, gain_pair, weight_qkv, weight_out, weight_up, weight_down):
    row_count = patch_rows.shape[0]
    head_size = D // HEADS
    residual = patch_rows.astype(jnp.float32)
    normal_in = normed(residual, gain_pair[0]).astype(jnp.bfloat16)
    joined = jnp.dot(normal_in, weight_qkv, preferred_element_type=jnp.float32).astype(jnp.bfloat16)
    queries = joined[:, :D].reshape(row_count, HEADS, head_size)
    keys_all = joined[:, D:2 * D].reshape(row_count, HEADS, head_size).astype(jnp.float32)
    values_all = joined[:, 2 * D:].reshape(row_count, HEADS, head_size).astype(jnp.float32)
    query_step = min(512, row_count)
    scaling = head_size ** (-0.5)

    def attend(query_block):
        scores = jnp.einsum('qhd,khd->hqk', query_block.astype(jnp.float32), keys_all) * scaling
        highest = lax.optimization_barrier(jnp.max(scores, axis=-1, keepdims=True))
        exponent = jnp.exp(scores - highest)
        weights = (exponent / lax.optimization_barrier(jnp.sum(exponent, axis=-1, keepdims=True))).astype(jnp.bfloat16)
        mixed = jnp.einsum('hqk,khd->qhd', weights.astype(jnp.float32), values_all)
        return mixed.astype(jnp.bfloat16)
    attended = lax.map(attend, queries.reshape(row_count // query_step, query_step, HEADS, head_size))
    attended = attended.reshape(row_count, D)
    after_attention = (residual + jnp.dot(attended, weight_out, preferred_element_type=jnp.float32)).astype(jnp.bfloat16)
    middle = after_attention.astype(jnp.float32)
    normal_mid = normed(middle, gain_pair[1]).astype(jnp.bfloat16)
    hidden = jax.nn.gelu(jnp.dot(normal_mid, weight_up, preferred_element_type=jnp.float32)).astype(jnp.bfloat16)
    return (middle + jnp.dot(hidden, weight_down, preferred_element_type=jnp.float32)).astype(jnp.bfloat16)

def apply_layer(current, layer_index, norm_gain, w_qkv, w_out, w_up, w_down):
    patches = current.reshape(DEVICES * PATCHES_DEV, PATCH, D)

    def single(patch_rows):
        return layer_patch(patch_rows, norm_gain[layer_index], w_qkv[layer_index], w_out[layer_index], w_up[layer_index], w_down[layer_index])
    return lax.map(single, patches).reshape(DEVICES, BLOCKS_DEV, BLOCK * D)

def reference(features, point_block, block_count, z_dest_dev, z_dest_slot, z_back_owner, z_back_block, hil_dest_dev, hil_dest_slot, hil_back_dev, hil_back_slot, norm_gain, w_qkv, w_out, w_up, w_down):
    points = features.reshape(DEVICES, ROWS, D)
    block_of_point = point_block.reshape(DEVICES, ROWS)
    positions = jnp.arange(ROWS, dtype=jnp.int32)
    ordering = jnp.argsort(block_of_point * ROWS + positions[None, :], axis=1).astype(jnp.int32)
    packed = jnp.take_along_axis(points, ordering[:, :, None], axis=1).reshape(DEVICES, CAP, BLOCK * D)
    devices = jnp.arange(DEVICES, dtype=jnp.int32)
    along_x = devices // N_GY
    along_y = devices % N_GY
    sources = (z_back_owner * N_GY + along_y[:, None]).astype(jnp.int32)
    current = packed[sources, z_back_block]
    current = apply_layer(current, 0, norm_gain, w_qkv, w_out, w_up, w_down)
    target = (along_x[:, None] * N_GY + hil_dest_dev).astype(jnp.int32)
    regrouped = jnp.zeros_like(current).at[target, hil_dest_slot].set(current)
    regrouped = apply_layer(regrouped, 1, norm_gain, w_qkv, w_out, w_up, w_down)
    target_back = (along_x[:, None] * N_GY + hil_back_dev).astype(jnp.int32)
    back_rows = jnp.zeros_like(regrouped).at[target_back, hil_back_slot].set(regrouped)
    holder = (z_dest_dev * N_GY + along_y[:, None]).astype(jnp.int32)
    at_home = back_rows[holder, z_dest_slot]
    alive = jnp.arange(CAP, dtype=jnp.int32)[None, :] < block_count[:, None]
    at_home = jnp.where(alive[:, :, None], at_home, jnp.zeros_like(at_home))
    in_order = at_home.reshape(DEVICES, ROWS, D)
    restored = jnp.zeros_like(in_order).at[devices[:, None], ordering].set(in_order)
    return restored.reshape(DEVICES * ROWS, D)
```

```python
import functools

import jax
import jax.numpy as jnp
from jax import lax
from jax.experimental import pallas as pl
from jax.experimental.pallas import tpu as pltpu
from jax.sharding import PartitionSpec as P

MESH = pl.DeviceIdType.MESH
D = 512
FF = 2048
BLOCK = 128
CAP = 16
SLOTS = 8
ROWS = CAP * BLOCK
CHUNKS = 4
STEP = BLOCK // CHUNKS
PART = SLOTS * STEP
LANES = 16
PAIRS = 4
EPSILON = 1e-05
BF = jnp.bfloat16
F32 = jnp.float32
SEND_SLOT, RECV_LANE, BACK_SLOT, HOME_LANE, FROM_LANE, OWN_BLOCK = 0, 16, 24, 40, 56, 64

GX_OFFSETS = (
    (0, 1), (1, 0), (0, 3), (3, 0), (1, 1), (3, 3), (1, 3), (3, 1),
    (2, 0), (0, 2), (2, 1), (1, 2), (2, 3), (3, 2), (2, 2),
)
GY_OFFSETS = ((1, 0), (3, 0), (2, 0), (1, 1), (3, 1), (2, 1), (0, 1))


def normed(values_in, gain_row):
    centered = values_in - jnp.mean(values_in, axis=-1, keepdims=True)
    variance = jnp.mean(centered * centered, axis=-1, keepdims=True)
    return centered * lax.rsqrt(variance + EPSILON) * gain_row


def gelu(x):
    inner = x * (0.7978845608028654 + 0.035677408136300125 * (x * x))
    return (0.5 * x) * (1.0 + jnp.tanh(inner))


def row_keys(blocks_of):
    groups = blocks_of.shape[0]
    masks = [jnp.where(blocks_of == b, 1.0, 0.0) for b in range(CAP)]
    stacked = jnp.concatenate(masks, axis=0)
    stacked_low = stacked.astype(BF)
    row = lax.broadcasted_iota(jnp.int32, (128, 128), 0)
    col = lax.broadcasted_iota(jnp.int32, (128, 128), 1)
    before = jnp.where(row < col, 1.0, 0.0).astype(BF)
    within = jnp.dot(stacked_low, before, preferred_element_type=F32)
    totals = jnp.dot(stacked_low, jnp.ones((128, 128), BF), preferred_element_type=F32).astype(BF)
    size = CAP * groups
    high = lax.broadcasted_iota(jnp.int32, (size, size), 0)
    low = lax.broadcasted_iota(jnp.int32, (size, size), 1)
    earlier = jnp.where((high // groups == low // groups) & (low < high), 1.0, 0.0).astype(BF)
    ahead = jnp.dot(earlier, totals, preferred_element_type=F32)
    ranks = within + ahead
    total = jnp.zeros((groups, 128), F32)
    for b in range(CAP):
        part = slice(b * groups, (b + 1) * groups)
        total = total + stacked[part] * (ranks[part] + float(b * BLOCK))
    return total


def kernel(
    table, blocks_ref, gain_ref, feat_h, wqkv_h, wout_h, wup_h, wdown_h, out_ref,
    feat, wqkv, wout, wup, wdown, keys, lanes_a, keys_wide, xs, q_s, k_s, v_s, y_s, lanes_1, lanes_2, lanes_b, arr_b,
    ax0, ax1, ax2, ax3, ay0, ay1, ay2, ay3, az0, az1, az2, az3,
    local_sem, send_a, recv_a, send_1, recv_1, send_2, recv_2, send_b, recv_b,
):
    arr_x = (ax0, ax1, ax2, ax3)
    arr_1 = (ay0, ay1, ay2, ay3)
    arr_2 = (az0, az1, az2, az3)
    gx = lax.axis_index("gx")
    gy = lax.axis_index("gy")
    z, y = gx // 4, gx % 4
    x, core = gy // 2, gy % 2
    gx_peers = [((z + dz) % 4) * 4 + (y + dy) % 4 for dz, dy in GX_OFFSETS]
    gx_sources = [((z + 4 - dz) % 4) * 4 + (y + 4 - dy) % 4 for dz, dy in GX_OFFSETS]
    gy_peers = [((x + dx) % 4) * 2 + (core + dc) % 2 for dx, dc in GY_OFFSETS]
    gy_sources = [((x + 4 - dx) % 4) * 2 + (core + dc) % 2 for dx, dc in GY_OFFSETS]

    loads = [pltpu.make_async_copy(feat_h, feat, local_sem.at[0])]
    for layer in range(2):
        for i, (src, dst) in enumerate(((wqkv_h, wqkv), (wout_h, wout), (wup_h, wup), (wdown_h, wdown))):
            loads.append(pltpu.make_async_copy(src.at[layer], dst.at[layer], local_sem.at[1 + layer * 4 + i]))
    for load in loads:
        load.start()

    barrier = pltpu.get_barrier_semaphore()
    for peer in gx_peers:
        pl.semaphore_signal(barrier, inc=1, device_id=(peer, gy), device_id_type=MESH)
    for peer in gy_peers:
        pl.semaphore_signal(barrier, inc=1, device_id=(gx, peer), device_id_type=MESH)

    def gx_copy(lanes, c, arrived, send, recv, peer, source):
        return pltpu.make_async_remote_copy(
            src_ref=lanes.at[c, peer], dst_ref=arrived.at[source],
            send_sem=send.at[c, peer], recv_sem=recv.at[c, source],
            device_id=(peer, gy), device_id_type=MESH,
        )

    def gy_copy(lanes, c, arrived, send, recv, peer, source):
        return pltpu.make_async_remote_copy(
            src_ref=lanes.at[c, pl.ds(peer * 2, 2)], dst_ref=arrived.at[pl.ds(source * 2, 2)],
            send_sem=send.at[c, peer], recv_sem=recv.at[c, source],
            device_id=(gx, peer), device_id_type=MESH,
        )

    key_rows = row_keys(blocks_ref[...])
    keys[...] = key_rows.astype(jnp.int32)
    padded = jnp.concatenate([key_rows, jnp.zeros((128 - 16, 128), F32)], axis=0)
    turned = padded.T.astype(jnp.int32)
    for g in range(16):
        keys_wide[g * 128 : (g + 1) * 128, :] = jnp.broadcast_to(turned[:, g : g + 1], (128, 128))

    loads[0].wait()
    for c in range(CHUNKS):
        for half in range(2):
            rows_in = lax.broadcasted_iota(jnp.int32, (STEP, 128), 0) + c * STEP
            wanted = jnp.concatenate(
                [rows_in + table[OWN_BLOCK + half * 8 + k] for k in range(8)], axis=0
            )
            picker = jnp.concatenate(
                [jnp.where(wanted == keys[g : g + 1, :], 1.0, 0.0).astype(BF) for g in range(16)], axis=1
            )
            packed = jnp.dot(picker, feat[...], preferred_element_type=F32).astype(BF)
            lanes_a[c, half * 8 : half * 8 + 8] = packed.reshape(8, STEP, D)
        if c == 0:
            pl.semaphore_wait(barrier, len(gx_peers) + len(gy_peers))
        for peer in gx_peers:
            gx_copy(lanes_a, c, arr_x[c], send_a, recv_a, peer, gx).start()
        arr_x[c][gx] = lanes_a[c, gx]

    lane_of = lax.broadcasted_iota(jnp.int32, (PART, 128), 1)
    low_half = lane_of < 64

    def project(layer, c):
        values = xs[c].astype(F32)
        normal = normed(values, gain_ref[layer, 0:1, :]).astype(BF)
        joined = jnp.dot(normal, wqkv[layer], preferred_element_type=F32)
        rows = pl.ds(c * PART, PART)
        for pair in range(PAIRS):
            q_s[pair, rows, :] = joined[:, pair * 128 : (pair + 1) * 128].astype(BF) * jnp.asarray(0.125, BF)
            k_s[pair, rows, :] = joined[:, D + pair * 128 : D + (pair + 1) * 128].astype(BF)
            v_s[pair, rows, 0:128] = joined[:, 2 * D + pair * 128 : 2 * D + (pair + 1) * 128].astype(BF)
            v_s[pair, rows, 128:256] = jnp.ones((PART, 128), BF)

    def finish(layer, c):
        rows = pl.ds(c * PART, PART)
        mixed = []
        for pair in range(PAIRS):
            q_pair = q_s[pair, rows, :]
            zero = jnp.zeros_like(q_pair)
            both = []
            for head in range(2):
                q_head = jnp.where(low_half, q_pair, zero) if head == 0 else jnp.where(low_half, zero, q_pair)
                scores = lax.dot_general(q_head, k_s[pair], (((1,), (1,)), ((), ())), preferred_element_type=F32)
                highest = jnp.max(scores, axis=-1, keepdims=True)
                weights = jnp.exp(scores - highest).astype(BF)
                summed = jnp.dot(weights, v_s[pair], preferred_element_type=F32)
                both.append(summed[:, 0:128] / summed[:, 128:256])
            mixed.append(jnp.where(low_half, both[0], both[1]).astype(BF))
        attended = jnp.concatenate(mixed, axis=1)
        after = (xs[c].astype(F32) + jnp.dot(attended, wout[layer], preferred_element_type=F32)).astype(BF)
        middle = after.astype(F32)
        normal = normed(middle, gain_ref[layer, 1:2, :]).astype(BF)
        total = middle
        for j in range(4):
            cols = slice(j * 512, (j + 1) * 512)
            hidden = gelu(jnp.dot(normal, wup[layer, :, cols], preferred_element_type=F32)).astype(BF)
            total = total + jnp.dot(hidden, wdown[layer, cols, :], preferred_element_type=F32)
        y_s[...] = total.astype(BF).reshape(SLOTS, STEP, D)

    def receive_and_project(layer, first, arrived, waits):
        def step(c, carry):
            for i in range(CHUNKS):
                @pl.when(c == i)
                def _():
                    waits(i)
                    for slot in range(SLOTS):
                        xs[i, slot * STEP : (slot + 1) * STEP, :] = arrived[i][table[first + slot]]
            project(layer, c)
            return carry
        lax.fori_loop(0, CHUNKS, step, 0)

    def wait_x(i):
        for source in gx_sources:
            gx_copy(lanes_a, i, arr_x[i], send_a, recv_a, source, source).wait_recv()

    loads[1].wait()
    receive_and_project(0, FROM_LANE, arr_x, wait_x)
    for load in loads[2:5]:
        load.wait()

    def compute_and_send(layer, first, lanes, arrived, send, recv, after):
        def step(c, carry):
            finish(layer, c)
            for lane in range(LANES):
                lanes[c, lane] = y_s[table[first + lane]]
            for i in range(CHUNKS):
                @pl.when(c == i)
                def _():
                    for peer in gy_peers:
                        gy_copy(lanes, i, arrived[i], send, recv, peer, gy).start()
                    for p in range(2):
                        arrived[i][gy * 2 + p] = lanes[i, gy * 2 + p]
                    after(i)
            return carry
        lax.fori_loop(0, CHUNKS, step, 0)

    compute_and_send(0, SEND_SLOT, lanes_1, arr_1, send_1, recv_1, lambda i: None)

    def wait_1(i):
        for source in gy_sources:
            gy_copy(lanes_1, i, arr_1[i], send_1, recv_1, source, source).wait_recv()

    loads[5].wait()
    receive_and_project(1, RECV_LANE, arr_1, wait_1)
    for load in loads[6:]:
        load.wait()

    def forward(i):
        for source in gy_sources:
            gy_copy(lanes_2, i, arr_2[i], send_2, recv_2, source, source).wait_recv()
        for k in range(LANES):
            lanes_b[i, k] = arr_2[i][table[HOME_LANE + k]]
        for peer in gx_peers:
            gx_copy(lanes_b, i, arr_b.at[i], send_b, recv_b, peer, gx).start()
        arr_b[i, gx] = lanes_b[i, gx]

    def after_2(i):
        if i >= 2:
            forward(i - 2)

    compute_and_send(1, BACK_SLOT, lanes_2, arr_2, send_2, recv_2, after_2)
    forward(2)

    quarter = lax.broadcasted_iota(jnp.int32, (1, 128), 1)

    def unpack(c, carry):
        for source in gx_sources:
            gx_copy(lanes_b, c, arr_b.at[c], send_b, recv_b, source, source).wait_recv()
        wanted = []
        for j in range(4):
            owned = [table[OWN_BLOCK + 4 * j + k] + c * STEP - STEP * k for k in range(4)]
            chosen = jnp.where(
                quarter < 2 * STEP,
                jnp.where(quarter < STEP, owned[0], owned[1]),
                jnp.where(quarter < 3 * STEP, owned[2], owned[3]),
            )
            wanted.append(chosen + quarter)
        landed = arr_b[c].reshape(LANES * STEP, D)
        for tile in range(4):
            rows = slice(tile * 512, (tile + 1) * 512)
            wide = keys_wide[rows, :]
            picker = jnp.concatenate([jnp.where(wide == w, 1.0, 0.0).astype(BF) for w in wanted], axis=1)
            part = jnp.dot(picker, landed, preferred_element_type=F32).astype(BF)

            @pl.when(c == 0)
            def _():
                out_ref[rows, :] = part

            @pl.when(c > 0)
            def _():
                out_ref[rows, :] = out_ref[rows, :] + part

        @pl.when(c == 0)
        def _():
            forward(3)
        return carry

    lax.fori_loop(0, CHUNKS, unpack, 0)

    for c in range(CHUNKS):
        for peer in gx_peers:
            gx_copy(lanes_a, c, arr_x[c], send_a, recv_a, peer, gx).wait_send()
            gx_copy(lanes_b, c, arr_b.at[c], send_b, recv_b, peer, gx).wait_send()
        for peer in gy_peers:
            gy_copy(lanes_1, c, arr_1[c], send_1, recv_1, peer, gy).wait_send()
            gy_copy(lanes_2, c, arr_2[c], send_2, recv_2, peer, gy).wait_send()


def rank_within(groups, order_key):
    same = groups[:, None] == groups[None, :]
    before = order_key[None, :] < order_key[:, None]
    return jnp.sum((same & before).astype(jnp.int32), axis=1)


def shards(
    features, point_block, block_count, z_dest_dev, z_dest_slot, z_back_owner, z_back_block,
    hil_dest_dev, hil_dest_slot, hil_back_dev, hil_back_slot, norm_gain, w_qkv, w_out, w_up, w_down,
):
    lanes = jnp.arange(LANES, dtype=jnp.int32)
    slots = jnp.arange(SLOTS, dtype=jnp.int32)
    alive = lanes < block_count[0]
    send_keys = hil_dest_dev[0] * 2 + rank_within(hil_dest_dev[0], slots)
    recv_keys = hil_back_dev[0] * 2 + rank_within(hil_back_dev[0], hil_back_slot[0])

    def placed(keys, values):
        hit = keys[None, :] == lanes[:, None]
        return jnp.sum(jnp.where(hit, values[None, :], 0), axis=1)

    owned = placed(jnp.where(alive, z_dest_dev[0], -1), lanes * BLOCK + 1000000) - 1000000
    table = jnp.concatenate(
        [
            placed(send_keys, slots),
            recv_keys,
            placed(recv_keys, slots),
            placed(z_back_owner[0], send_keys),
            z_back_owner[0],
            owned,
        ]
    ).astype(jnp.int32)

    any_space = pl.BlockSpec(memory_space=pl.ANY)
    vmem = pl.BlockSpec(memory_space=pltpu.VMEM)
    dma = pltpu.SemaphoreType.DMA
    landing = [pltpu.VMEM((LANES, STEP, D), BF) for _ in range(3 * CHUNKS)]
    return pl.pallas_call(
        kernel,
        out_shape=jax.ShapeDtypeStruct((ROWS, D), BF),
        in_specs=[pl.BlockSpec(memory_space=pltpu.SMEM), vmem, vmem] + [any_space] * 5,
        out_specs=vmem,
        scratch_shapes=[
            pltpu.VMEM((ROWS, D), BF),
            pltpu.VMEM((2, D, 3 * D), BF),
            pltpu.VMEM((2, D, D), BF),
            pltpu.VMEM((2, D, FF), BF),
            pltpu.VMEM((2, FF, D), BF),
            pltpu.VMEM((16, 128), jnp.int32),
            pltpu.VMEM((CHUNKS, LANES, STEP, D), BF),
            pltpu.VMEM((ROWS, 128), jnp.int32),
            pltpu.VMEM((CHUNKS, PART, D), BF),
            pltpu.VMEM((PAIRS, CHUNKS * PART, 128), BF),
            pltpu.VMEM((PAIRS, CHUNKS * PART, 128), BF),
            pltpu.VMEM((PAIRS, CHUNKS * PART, 256), BF),
            pltpu.VMEM((SLOTS, STEP, D), BF),
            pltpu.VMEM((CHUNKS, LANES, STEP, D), BF),
            pltpu.VMEM((CHUNKS, LANES, STEP, D), BF),
            pltpu.VMEM((CHUNKS, LANES, STEP, D), BF),
            pltpu.VMEM((CHUNKS, LANES, STEP, D), BF),
        ]
        + landing
        + [
            dma((9,)),
            dma((CHUNKS, 16)), dma((CHUNKS, 16)), dma((CHUNKS, 8)), dma((CHUNKS, 8)),
            dma((CHUNKS, 8)), dma((CHUNKS, 8)), dma((CHUNKS, 16)), dma((CHUNKS, 16)),
        ],
        compiler_params=pltpu.CompilerParams(
            collective_id=0, has_side_effects=True, vmem_limit_bytes=63 * 1024 * 1024
        ),
    )(table, point_block.reshape(16, 128), norm_gain, features, w_qkv, w_out, w_up, w_down)


def solution(mesh):
    split = P(("gx", "gy"), None)
    flat = P(("gx", "gy"))
    in_specs = (split, flat, flat) + (split,) * 8 + (P(),) * 5
    return jax.shard_map(shards, mesh=mesh, in_specs=in_specs, out_specs=split, check_vma=False)
```

```python
import contextlib

import jax
import jax.numpy as jnp
from jax import lax
from jax.experimental import pallas as pl
from jax.experimental.pallas import tpu as pltpu
from jax.sharding import PartitionSpec as P

MESH = pl.DeviceIdType.MESH


def scope(name):
    return contextlib.nullcontext()


D = 512
FF = 2048
BLOCK = 128
CAP = 16
SLOTS = 8
ROWS = CAP * BLOCK
CHUNKS = 4
STEP = BLOCK // CHUNKS
PART = SLOTS * STEP
FINE = 8
FINE_STEP = BLOCK // FINE
LANES = 16
PAIRS = 4
EPSILON = 1e-05
BF = jnp.bfloat16
F32 = jnp.float32
SEND_SLOT, RECV_LANE, BACK_SLOT, HOME_LANE, FROM_LANE, OWN_BLOCK = 0, 16, 24, 40, 56, 64
NOWHERE = -1000000

GX_OFFSETS = (
    (0, 1), (1, 0), (0, 3), (3, 0), (1, 1), (3, 3), (1, 3), (3, 1),
    (2, 0), (0, 2), (2, 1), (1, 2), (2, 3), (3, 2), (2, 2),
)
GY_OFFSETS = ((1, 0), (3, 0), (2, 0), (1, 1), (3, 1), (2, 1), (0, 1))


def normed(values_in, gain_row):
    centered = values_in - jnp.mean(values_in, axis=-1, keepdims=True)
    variance = jnp.mean(centered * centered, axis=-1, keepdims=True)
    return centered * lax.rsqrt(variance + EPSILON) * gain_row


def gelu(x):
    inner = x * (0.7978845608028654 + 0.035677408136300125 * (x * x))
    return (0.5 * x) * (1.0 + jnp.tanh(inner))


def row_keys(blocks_of):
    groups = blocks_of.shape[0]
    masks = [jnp.where(blocks_of == b, 1.0, 0.0) for b in range(CAP)]
    stacked = jnp.concatenate(masks, axis=0)
    stacked_low = stacked.astype(BF)
    row = lax.broadcasted_iota(jnp.int32, (128, 128), 0)
    col = lax.broadcasted_iota(jnp.int32, (128, 128), 1)
    before = jnp.where(row < col, 1.0, 0.0).astype(BF)
    within = jnp.dot(stacked_low, before, preferred_element_type=F32)
    totals = jnp.dot(stacked_low, jnp.ones((128, 128), BF), preferred_element_type=F32).astype(BF)
    size = CAP * groups
    high = lax.broadcasted_iota(jnp.int32, (size, size), 0)
    low = lax.broadcasted_iota(jnp.int32, (size, size), 1)
    earlier = jnp.where((high // groups == low // groups) & (low < high), 1.0, 0.0).astype(BF)
    ahead = jnp.dot(earlier, totals, preferred_element_type=F32)
    ranks = within + ahead
    total = jnp.zeros((groups, 128), F32)
    for b in range(CAP):
        part = slice(b * groups, (b + 1) * groups)
        total = total + stacked[part] * (ranks[part] + float(b * BLOCK))
    return total


def own_table(table, counts, z_dest):
    dests = [jnp.where(b < counts[0], z_dest[0, b], -1) for b in range(CAP)]
    for lane in range(LANES):
        chosen = jnp.int32(NOWHERE)
        for b in range(CAP):
            chosen = jnp.where(dests[b] == lane, b * BLOCK, chosen)
        table[OWN_BLOCK + lane] = chosen


def move_tables(table, z_owner, h_dest, h_back, h_slot):
    dest = [h_dest[0, s] for s in range(SLOTS)]
    back = [h_back[0, s] for s in range(SLOTS)]
    slot = [h_slot[0, s] for s in range(SLOTS)]
    owner = [z_owner[0, s] for s in range(SLOTS)]
    send_keys = []
    recv_keys = []
    for s in range(SLOTS):
        key = dest[s] * 2
        for other in range(s):
            key = key + jnp.where(dest[other] == dest[s], 1, 0)
        send_keys.append(key)
        key = back[s] * 2
        for other in range(SLOTS):
            if other != s:
                key = key + jnp.where((back[other] == back[s]) & (slot[other] < slot[s]), 1, 0)
        recv_keys.append(key)
        table[RECV_LANE + s] = key
        table[FROM_LANE + s] = owner[s]
    for lane in range(LANES):
        send = jnp.int32(0)
        back_slot = jnp.int32(0)
        home = jnp.int32(0)
        for s in range(SLOTS):
            send = jnp.where(send_keys[s] == lane, s, send)
            back_slot = jnp.where(recv_keys[s] == lane, s, back_slot)
            home = jnp.where(owner[s] == lane, send_keys[s], home)
        table[SEND_SLOT + lane] = send
        table[BACK_SLOT + lane] = back_slot
        table[HOME_LANE + lane] = home


def kernel(
    counts, z_dest, z_owner, h_dest, h_back, h_slot,
    blocks_ref, gain_ref, feat_h, wqkv_h, wout_h, wup_h, wdown_h, out_ref,
    table, feat, wqkv, wout, wup, wdown, keys, lanes_a, keys_wide, xs, q_s, k_s, v_s, mid_s, y_s, lanes_1, lanes_2, lanes_b, arr_b,
    *rest,
):
    arr_x, arr_1, arr_2 = rest[:CHUNKS], rest[CHUNKS : CHUNKS + FINE], rest[CHUNKS + FINE : CHUNKS + 2 * FINE]
    local_sem, send_a, recv_a, send_1, recv_1, send_2, recv_2, send_b, recv_b = rest[CHUNKS + 2 * FINE :]
    gx = lax.axis_index("gx")
    gy = lax.axis_index("gy")
    z, y = gx // 4, gx % 4
    x, core = gy // 2, gy % 2
    gx_peers = [((z + dz) % 4) * 4 + (y + dy) % 4 for dz, dy in GX_OFFSETS]
    gy_peers = [((x + dx) % 4) * 2 + (core + dc) % 2 for dx, dc in GY_OFFSETS]

    loads = [pltpu.make_async_copy(feat_h, feat, local_sem.at[0])]
    for layer in range(2):
        for i, (src, dst) in enumerate(((wqkv_h, wqkv), (wout_h, wout), (wup_h, wup), (wdown_h, wdown))):
            loads.append(pltpu.make_async_copy(src.at[layer], dst.at[layer], local_sem.at[1 + layer * 4 + i]))
    for load in loads:
        load.start()

    barrier = pltpu.get_barrier_semaphore()
    for peer in gx_peers:
        pl.semaphore_signal(barrier, inc=1, device_id=(peer, gy), device_id_type=MESH)
    for peer in gy_peers:
        pl.semaphore_signal(barrier, inc=1, device_id=(gx, peer), device_id_type=MESH)

    def gx_copy(src, dst, send, recv, peer):
        return pltpu.make_async_remote_copy(
            src_ref=src, dst_ref=dst, send_sem=send, recv_sem=recv, device_id=(peer, gy), device_id_type=MESH,
        )

    def gy_copy(src, dst, send, recv, peer):
        return pltpu.make_async_remote_copy(
            src_ref=src, dst_ref=dst, send_sem=send, recv_sem=recv, device_id=(gx, peer), device_id_type=MESH,
        )

    def gx_all(lanes, c, arrived, send, recv):
        part = pl.ds(0, LANES - 1)
        return gx_copy(lanes.at[c, part], arrived.at[part], send.at[c], recv.at[c], gx_peers[0])

    def gy_all(lanes, c, arrived, send, recv):
        part = pl.ds(0, LANES - 2)
        return gy_copy(lanes.at[c, part], arrived.at[part], send.at[c], recv.at[c], gy_peers[0])

    own_table(table, counts, z_dest)
    with scope('keys'):
        key_rows = row_keys(blocks_ref[...])
    keys[...] = key_rows.astype(jnp.int32)
    with scope('ldw'):
        loads[0].wait()
    for c in range(CHUNKS):
        group = 256 // STEP
        for first in range(0, LANES, group):
            rows_in = lax.broadcasted_iota(jnp.int32, (STEP, 128), 0) + c * STEP
            wanted = jnp.concatenate(
                [rows_in + table[OWN_BLOCK + first + k] for k in range(group)], axis=0
            )
            picker = jnp.concatenate(
                [jnp.where(wanted == keys[g : g + 1, :], 1.0, 0.0).astype(BF) for g in range(16)], axis=1
            )
            with scope('pack'):
                packed = jnp.dot(picker, feat[...], preferred_element_type=F32).astype(BF)
            lanes_a[c, first : first + group] = packed.reshape(group, STEP, D)
        if c == 0:
            with scope('barr'):
                pl.semaphore_wait(barrier, len(gx_peers) + len(gy_peers))
        for peer in gx_peers:
            gx_copy(lanes_a.at[c, peer], arr_x[c].at[gx], send_a.at[c], recv_a.at[c], peer).start()
        arr_x[c][gx] = lanes_a[c, gx]

    with scope('mov'):
        move_tables(table, z_owner, h_dest, h_back, h_slot)
    padded = jnp.concatenate([key_rows, jnp.zeros((128 - 16, 128), F32)], axis=0)
    turned = padded.T.astype(jnp.int32)
    for g in range(16):
        keys_wide[g * 128 : (g + 1) * 128, :] = jnp.broadcast_to(turned[:, g : g + 1], (128, 128))


    def project(layer, c):
        rows = pl.ds(c * PART, PART)
        values = xs[rows, :].astype(F32)
        normal = normed(values, gain_ref[layer, 0:1, :]).astype(BF)
        joined = jnp.dot(normal, wqkv[layer], preferred_element_type=F32)
        for pair in range(PAIRS):
            q_s[pair, rows, :] = joined[:, pair * 128 : (pair + 1) * 128].astype(BF) * jnp.asarray(0.125, BF)
            k_s[pair, rows, :] = joined[:, D + pair * 128 : D + (pair + 1) * 128].astype(BF)
            v_s[pair, rows, 0:128] = joined[:, 2 * D + pair * 128 : 2 * D + (pair + 1) * 128].astype(BF)
            v_s[pair, rows, 128:256] = jnp.ones((PART, 128), BF)

    def attend(layer, c):
        part = SLOTS * FINE_STEP
        rows = pl.ds(c * part, part)
        low_half = lax.broadcasted_iota(jnp.int32, (part, 128), 1) < 64
        mixed = []
        for pair in range(PAIRS):
            q_pair = q_s[pair, rows, :]
            zero = jnp.zeros_like(q_pair)
            both = jnp.concatenate([jnp.where(low_half, q_pair, zero), jnp.where(low_half, zero, q_pair)], axis=0)
            scores = lax.dot_general(both, k_s[pair], (((1,), (1,)), ((), ())), preferred_element_type=F32)
            highest = jnp.max(scores, axis=-1, keepdims=True)
            weights = jnp.exp(scores - highest).astype(BF)
            summed = jnp.dot(weights, v_s[pair], preferred_element_type=F32)
            chosen = jnp.where(low_half, summed[:part, 0:128], summed[part:, 0:128])
            divisor = jnp.where(low_half, summed[:part, 128:256], summed[part:, 128:256])
            mixed.append((chosen / divisor).astype(BF))
            yield None
        attended = jnp.concatenate(mixed, axis=1)
        yield (xs[rows, :].astype(F32) + jnp.dot(attended, wout[layer], preferred_element_type=F32)).astype(BF)

    def feed_forward(layer, after):
        middle = after.astype(F32)
        normal = normed(middle, gain_ref[layer, 1:2, :]).astype(BF)
        total = middle
        for j in range(4):
            cols = slice(j * 512, (j + 1) * 512)
            hidden = gelu(jnp.dot(normal, wup[layer, :, cols], preferred_element_type=F32)).astype(BF)
            total = total + jnp.dot(hidden, wdown[layer, cols, :], preferred_element_type=F32)
            yield None
        yield total.astype(BF).reshape(SLOTS, FINE_STEP, D)

    def receive_and_project(layer, waits, block_of):
        def body(c, carry):
            for i in range(CHUNKS):
                @pl.when(c == i)
                def _():
                    with scope('wait'):
                        waits(i)
                    for slot in range(SLOTS):
                        for j, piece in enumerate(block_of(i, slot)):
                            at = i * PART + j * SLOTS * FINE_STEP + slot * FINE_STEP
                            xs[at : at + FINE_STEP, :] = piece
            with scope('proj'):
                project(layer, c)
            return carry
        lax.fori_loop(0, CHUNKS, body, 0)

    fold = FINE // CHUNKS

    def wait_x(i):
        gx_all(lanes_a, i, arr_x[i], send_a, recv_a).wait_recv()

    def block_x(i, slot):
        block = arr_x[i][table[FROM_LANE + slot]]
        return [block[j * FINE_STEP : (j + 1) * FINE_STEP, :] for j in range(fold)]

    def wait_1(i):
        for j in range(i * fold, i * fold + fold):
            gy_all(lanes_1, j, arr_1[j], send_1, recv_1).wait_recv()

    def block_1(i, slot):
        return [arr_1[j][table[RECV_LANE + slot]] for j in range(i * fold, i * fold + fold)]

    def forward(i):
        with scope('waitG2'):
            gy_all(lanes_2, i, arr_2[i], send_2, recv_2).wait_recv()
        for k in range(LANES):
            lanes_b[i, k] = arr_2[i][table[HOME_LANE + k]]
        for peer in gx_peers:
            gx_copy(lanes_b.at[i, peer], arr_b.at[i, gx], send_b.at[i], recv_b.at[i], peer).start()
        arr_b[i, gx] = lanes_b[i, gx]

    def compute_and_send(layer, first, lanes, arrived, send, recv, meanwhile):
        def deliver(i):
            for peer in gy_peers:
                pair = pl.ds(peer * 2, 2)
                gy_copy(lanes.at[i, pair], arrived[i].at[pl.ds(gy * 2, 2)], send.at[i], recv.at[i], peer).start()
            for p in range(2):
                arrived[i][gy * 2 + p] = lanes[i, gy * 2 + p]

        def fill(c):
            for lane in range(LANES):
                lanes[c, lane] = y_s[table[first + lane]]

        with scope('att'):
            mid_s[...] = list(attend(layer, 0))[-1]

        def body(c, carry):
            with scope('both'):
                lower = feed_forward(layer, mid_s[...])
                for upper in attend(layer, c + 1):
                    done = next(lower)
                mid_s[...] = upper
                y_s[...] = done
            fill(c)
            for i in range(FINE - 1):
                @pl.when(c == i)
                def _():
                    deliver(i)
                    if meanwhile is not None and i >= 2:
                        meanwhile(i - 2)
            return carry
        lax.fori_loop(0, FINE - 1, body, 0)
        with scope('mlp'):
            y_s[...] = list(feed_forward(layer, mid_s[...]))[-1]
        fill(FINE - 1)
        deliver(FINE - 1)

    loads[1].wait()
    receive_and_project(0, wait_x, block_x)
    for load in loads[2:5]:
        load.wait()
    compute_and_send(0, SEND_SLOT, lanes_1, arr_1, send_1, recv_1, None)
    loads[5].wait()
    receive_and_project(1, wait_1, block_1)
    for load in loads[6:]:
        load.wait()
    compute_and_send(1, BACK_SLOT, lanes_2, arr_2, send_2, recv_2, forward)

    quarter = lax.broadcasted_iota(jnp.int32, (1, 128), 1)

    def unpack(c, carry):
        with scope('waitB'):
            for j in range(fold):
                i = c * fold + j
                gx_all(lanes_b, i, arr_b.at[i], send_b, recv_b).wait_recv()
        wanted = []
        count = 128 // FINE_STEP
        for j in range(fold):
            shift = (c * fold + j) * FINE_STEP
            for first in range(0, LANES, count):
                chosen = jnp.full((1, 128), table[OWN_BLOCK + first] + shift, jnp.int32)
                for k in range(1, count):
                    lane_key = table[OWN_BLOCK + first + k] + shift - k * FINE_STEP
                    chosen = jnp.where(quarter < k * FINE_STEP, chosen, lane_key)
                wanted.append(chosen + quarter)
        landed = arr_b[pl.ds(c * fold, fold)].reshape(fold * LANES * FINE_STEP, D)
        for tile in range(4):
            rows = slice(tile * 512, (tile + 1) * 512)
            wide = keys_wide[rows, :]
            picker = jnp.concatenate([jnp.where(wide == w, 1.0, 0.0).astype(BF) for w in wanted], axis=1)
            with scope('unp'):
                part = jnp.dot(picker, landed, preferred_element_type=F32).astype(BF)
            if isinstance(c, int):
                out_ref[rows, :] = part
            else:
                out_ref[rows, :] = out_ref[rows, :] + part
        return carry

    forward(FINE - 3)
    forward(FINE - 2)
    unpack(0, 0)
    forward(FINE - 1)
    lax.fori_loop(1, CHUNKS, unpack, 0)

    for c in range(CHUNKS):
        gx_all(lanes_a, c, arr_x[c], send_a, recv_a).wait_send()
    for c in range(FINE):
        gy_all(lanes_1, c, arr_1[c], send_1, recv_1).wait_send()
        gy_all(lanes_2, c, arr_2[c], send_2, recv_2).wait_send()
        gx_all(lanes_b, c, arr_b.at[c], send_b, recv_b).wait_send()


def shards(
    features, point_block, block_count, z_dest_dev, z_dest_slot, z_back_owner, z_back_block,
    hil_dest_dev, hil_dest_slot, hil_back_dev, hil_back_slot, norm_gain, w_qkv, w_out, w_up, w_down,
):
    any_space = pl.BlockSpec(memory_space=pl.ANY)
    vmem = pl.BlockSpec(memory_space=pltpu.VMEM)
    dma = pltpu.SemaphoreType.DMA
    landing = [pltpu.VMEM((LANES, STEP, D), BF) for _ in range(CHUNKS)]
    landing += [pltpu.VMEM((LANES, FINE_STEP, D), BF) for _ in range(2 * FINE)]
    return pl.pallas_call(
        kernel,
        out_shape=jax.ShapeDtypeStruct((ROWS, D), BF),
        in_specs=[pl.BlockSpec(memory_space=pltpu.SMEM)] * 6 + [vmem, vmem] + [any_space] * 5,
        out_specs=vmem,
        scratch_shapes=[
            pltpu.SMEM((80,), jnp.int32),
            pltpu.VMEM((ROWS, D), BF),
            pltpu.VMEM((2, D, 3 * D), BF),
            pltpu.VMEM((2, D, D), BF),
            pltpu.VMEM((2, D, FF), BF),
            pltpu.VMEM((2, FF, D), BF),
            pltpu.VMEM((16, 128), jnp.int32),
            pltpu.VMEM((CHUNKS, LANES, STEP, D), BF),
            pltpu.VMEM((ROWS, 128), jnp.int32),
            pltpu.VMEM((SLOTS * BLOCK, D), BF),
            pltpu.VMEM((PAIRS, SLOTS * BLOCK, 128), BF),
            pltpu.VMEM((PAIRS, SLOTS * BLOCK, 128), BF),
            pltpu.VMEM((PAIRS, SLOTS * BLOCK, 256), BF),
            pltpu.VMEM((SLOTS * FINE_STEP, D), BF),
            pltpu.VMEM((SLOTS, FINE_STEP, D), BF),
            pltpu.VMEM((FINE, LANES, FINE_STEP, D), BF),
            pltpu.VMEM((FINE, LANES, FINE_STEP, D), BF),
            pltpu.VMEM((FINE, LANES, FINE_STEP, D), BF),
            pltpu.VMEM((FINE, LANES, FINE_STEP, D), BF),
        ]
        + landing
        + [
            dma((9,)),
            dma((CHUNKS,)), dma((CHUNKS,)), dma((FINE,)), dma((FINE,)),
            dma((FINE,)), dma((FINE,)), dma((FINE,)), dma((FINE,)),
        ],
        compiler_params=pltpu.CompilerParams(
            collective_id=0, has_side_effects=True, vmem_limit_bytes=63 * 1024 * 1024
        ),
    )(
        block_count, z_dest_dev, z_back_owner, hil_dest_dev, hil_back_dev, hil_back_slot,
        point_block.reshape(16, 128), norm_gain, features, w_qkv, w_out, w_up, w_down,
    )


def solution(mesh):
    split = P(("gx", "gy"), None)
    flat = P(("gx", "gy"))
    in_specs = (split, flat, flat) + (split,) * 8 + (P(),) * 5
    return jax.shard_map(shards, mesh=mesh, in_specs=in_specs, out_specs=split, check_vma=False)
```

```python
import contextlib

import jax
import jax.numpy as jnp
from jax import lax
from jax.experimental import pallas as pl
from jax.experimental.pallas import tpu as pltpu
from jax.sharding import PartitionSpec as P

MESH = pl.DeviceIdType.MESH


def scope(name):
    return contextlib.nullcontext()


D = 512
FF = 2048
BLOCK = 128
CAP = 16
SLOTS = 8
ROWS = CAP * BLOCK
CHUNKS = 4
STEP = BLOCK // CHUNKS
PART = SLOTS * STEP
FINE = 8
FINE_STEP = BLOCK // FINE
LANES = 16
PAIRS = 4
EPSILON = 1e-05
BF = jnp.bfloat16
F32 = jnp.float32
SEND_SLOT, RECV_LANE, BACK_SLOT, HOME_LANE, FROM_LANE, OWN_BLOCK = 0, 16, 24, 40, 56, 64
NOWHERE = -1000000

GX_OFFSETS = (
    (0, 1), (1, 0), (0, 3), (3, 0), (1, 1), (3, 3), (1, 3), (3, 1),
    (2, 0), (0, 2), (2, 1), (1, 2), (2, 3), (3, 2), (2, 2),
)
GY_OFFSETS = ((1, 0), (3, 0), (2, 0), (1, 1), (3, 1), (2, 1), (0, 1))


def normed(values_in, gain_row):
    centered = values_in - jnp.mean(values_in, axis=-1, keepdims=True)
    variance = jnp.mean(centered * centered, axis=-1, keepdims=True)
    return centered * lax.rsqrt(variance + EPSILON) * gain_row


def gelu(x):
    inner = x * (0.7978845608028654 + 0.035677408136300125 * (x * x))
    return (0.5 * x) * (1.0 + jnp.tanh(inner))


def row_keys(blocks_of):
    groups = blocks_of.shape[0]
    masks = [jnp.where(blocks_of == b, 1.0, 0.0) for b in range(CAP)]
    stacked = jnp.concatenate(masks, axis=0)
    stacked_low = stacked.astype(BF)
    row = lax.broadcasted_iota(jnp.int32, (128, 128), 0)
    col = lax.broadcasted_iota(jnp.int32, (128, 128), 1)
    before = jnp.where(row < col, 1.0, 0.0).astype(BF)
    within = jnp.dot(stacked_low, before, preferred_element_type=F32)
    totals = jnp.dot(stacked_low, jnp.ones((128, 128), BF), preferred_element_type=F32).astype(BF)
    size = CAP * groups
    high = lax.broadcasted_iota(jnp.int32, (size, size), 0)
    low = lax.broadcasted_iota(jnp.int32, (size, size), 1)
    earlier = jnp.where((high // groups == low // groups) & (low < high), 1.0, 0.0).astype(BF)
    ahead = jnp.dot(earlier, totals, preferred_element_type=F32)
    ranks = within + ahead
    total = jnp.zeros((groups, 128), F32)
    for b in range(CAP):
        part = slice(b * groups, (b + 1) * groups)
        total = total + stacked[part] * (ranks[part] + float(b * BLOCK))
    return total


def own_table(table, counts, z_dest):
    live = counts[0]
    dests = [jnp.where(b < live, z_dest[0, b], -1) for b in range(CAP)]
    for lane in range(LANES):
        chosen = jnp.int32(NOWHERE)
        for b in range(CAP):
            chosen = jnp.where(dests[b] == lane, b * BLOCK, chosen)
        table[OWN_BLOCK + lane] = chosen


def move_tables(table, z_owner, h_dest, h_back, h_slot):
    dest = [h_dest[0, s] for s in range(SLOTS)]
    back = [h_back[0, s] for s in range(SLOTS)]
    slot = [h_slot[0, s] for s in range(SLOTS)]
    owner = [z_owner[0, s] for s in range(SLOTS)]
    send_keys = []
    recv_keys = []
    for s in range(SLOTS):
        key = dest[s] * 2
        for other in range(s):
            key = key + jnp.where(dest[other] == dest[s], 1, 0)
        send_keys.append(key)
        key = back[s] * 2
        for other in range(SLOTS):
            if other != s:
                key = key + jnp.where((back[other] == back[s]) & (slot[other] < slot[s]), 1, 0)
        recv_keys.append(key)
        table[RECV_LANE + s] = key
        table[FROM_LANE + s] = owner[s]
    for lane in range(LANES):
        send = jnp.int32(0)
        back_slot = jnp.int32(0)
        home = jnp.int32(0)
        for s in range(SLOTS):
            send = jnp.where(send_keys[s] == lane, s, send)
            back_slot = jnp.where(recv_keys[s] == lane, s, back_slot)
            home = jnp.where(owner[s] == lane, send_keys[s], home)
        table[SEND_SLOT + lane] = send
        table[BACK_SLOT + lane] = back_slot
        table[HOME_LANE + lane] = home


def kernel(
    counts, z_dest_h, z_owner_h, h_dest_h, h_back_h, h_slot_h, blocks_h, gain_h,
    feat_h, wqkv_h, wout_h, wup_h, wdown_h, out_ref,
    z_dest, z_owner, h_dest, h_back, h_slot, blocks_ref, gain_ref,
    table, feat, wqkv, wout, wup, wdown, keys, lanes_a, keys_wide, pick_s, xs, q_s, k_s, v_s, mid_s, y_s, lanes_1, lanes_2, lanes_b, arr_b,
    *rest,
):
    arr_x, arr_1, arr_2 = rest[:CHUNKS], rest[CHUNKS : CHUNKS + FINE], rest[CHUNKS + FINE : CHUNKS + 2 * FINE]
    local_sem, send_a, recv_a, send_1, recv_1, send_2, recv_2, send_b, recv_b = rest[CHUNKS + 2 * FINE :]
    gx = lax.axis_index("gx")
    gy = lax.axis_index("gy")
    z, y = gx // 4, gx % 4
    x, core = gy // 2, gy % 2
    gx_peers = [((z + dz) % 4) * 4 + (y + dy) % 4 for dz, dy in GX_OFFSETS]
    gy_peers = [((x + dx) % 4) * 2 + (core + dc) % 2 for dx, dc in GY_OFFSETS]

    barrier = pltpu.get_barrier_semaphore()
    for peer in gx_peers:
        pl.semaphore_signal(barrier, inc=1, device_id=(peer, gy), device_id_type=MESH)
    for peer in gy_peers:
        pl.semaphore_signal(barrier, inc=1, device_id=(gx, peer), device_id_type=MESH)

    small = []
    for i, (src, dst) in enumerate(
        (
            (blocks_h, blocks_ref), (z_dest_h, z_dest), (z_owner_h, z_owner),
            (h_dest_h, h_dest), (h_back_h, h_back), (h_slot_h, h_slot), (gain_h, gain_ref),
        )
    ):
        small.append(pltpu.make_async_copy(src, dst, local_sem.at[9 + i]))
    for load in small:
        load.start()
    loads = [pltpu.make_async_copy(feat_h, feat, local_sem.at[0])]
    for layer in range(2):
        for i, (src, dst) in enumerate(((wqkv_h, wqkv), (wout_h, wout), (wup_h, wup), (wdown_h, wdown))):
            loads.append(pltpu.make_async_copy(src.at[layer], dst.at[layer], local_sem.at[1 + layer * 4 + i]))
    for load in loads:
        load.start()

    def gx_copy(src, dst, send, recv, peer):
        return pltpu.make_async_remote_copy(
            src_ref=src, dst_ref=dst, send_sem=send, recv_sem=recv, device_id=(peer, gy), device_id_type=MESH,
        )

    def gy_copy(src, dst, send, recv, peer):
        return pltpu.make_async_remote_copy(
            src_ref=src, dst_ref=dst, send_sem=send, recv_sem=recv, device_id=(gx, peer), device_id_type=MESH,
        )

    def gx_all(lanes, c, arrived, send, recv):
        part = pl.ds(0, LANES - 1)
        return gx_copy(lanes.at[c, part], arrived.at[part], send.at[c], recv.at[c], gx_peers[0])

    def gy_all(lanes, c, arrived, send, recv):
        part = pl.ds(0, LANES - 2)
        return gy_copy(lanes.at[c, part], arrived.at[part], send.at[c], recv.at[c], gy_peers[0])

    for load in small[:2]:
        load.wait()
    own_table(table, counts, z_dest)
    with scope('keys'):
        key_rows = row_keys(blocks_ref[...])
    keys[...] = key_rows.astype(jnp.int32)
    with scope('ldw'):
        loads[0].wait()
    order = gx_peers + [gx]
    for c in range(CHUNKS):
        group = 256 // STEP
        for first in range(0, LANES, group):
            rows_in = lax.broadcasted_iota(jnp.int32, (STEP, 128), 0) + c * STEP
            wanted = jnp.concatenate(
                [rows_in + table[OWN_BLOCK + order[first + k]] for k in range(group)], axis=0
            )
            picker = jnp.concatenate(
                [jnp.where(wanted == keys[g : g + 1, :], 1.0, 0.0).astype(BF) for g in range(16)], axis=1
            )
            with scope('pack'):
                packed = jnp.dot(picker, feat[...], preferred_element_type=F32).astype(BF)
            lanes_a[c, first : first + group] = packed.reshape(group, STEP, D)
            if c == 0 and first == 0:
                with scope('barr'):
                    pl.semaphore_wait(barrier, len(gx_peers) + len(gy_peers))
            for k in range(first, min(first + group, LANES - 1)):
                gx_copy(lanes_a.at[c, k], arr_x[c].at[gx], send_a.at[c], recv_a.at[c], order[k]).start()
        arr_x[c][gx] = lanes_a[c, LANES - 1]

    for load in small[2:]:
        load.wait()
    with scope('mov'):
        move_tables(table, z_owner, h_dest, h_back, h_slot)
    padded = jnp.concatenate([key_rows, jnp.zeros((128 - 16, 128), F32)], axis=0)
    turned = padded.T.astype(jnp.int32)
    for g in range(16):
        keys_wide[g * 128 : (g + 1) * 128, :] = jnp.broadcast_to(turned[:, g : g + 1], (128, 128))


    fold = FINE // CHUNKS

    def project(layer, c):
        rows = pl.ds(c * PART, PART)
        values = xs[rows, :].astype(F32)
        normal = normed(values, gain_ref[layer, 0:1, :]).astype(BF)
        joined = jnp.dot(normal, wqkv[layer], preferred_element_type=F32)
        for pair in range(PAIRS):
            q_s[pair, rows, :] = joined[:, pair * 128 : (pair + 1) * 128].astype(BF) * jnp.asarray(0.125, BF)
            k_s[pair, rows, :] = joined[:, D + pair * 128 : D + (pair + 1) * 128].astype(BF)
            v_s[pair, rows, 0:128] = joined[:, 2 * D + pair * 128 : 2 * D + (pair + 1) * 128].astype(BF)
            v_s[pair, rows, 128:256] = jnp.ones((PART, 128), BF)

    def attend(layer, c):
        part = SLOTS * FINE_STEP
        rows = pl.ds(c * part, part)
        low_half = lax.broadcasted_iota(jnp.int32, (part, 128), 1) < 64
        mixed = []
        for pair in range(PAIRS):
            q_pair = q_s[pair, rows, :]
            zero = jnp.zeros_like(q_pair)
            both = jnp.concatenate([jnp.where(low_half, q_pair, zero), jnp.where(low_half, zero, q_pair)], axis=0)
            scores = lax.dot_general(both, k_s[pair], (((1,), (1,)), ((), ())), preferred_element_type=F32)
            highest = jnp.max(scores, axis=-1, keepdims=True)
            weights = jnp.exp(scores - highest).astype(BF)
            summed = jnp.dot(weights, v_s[pair], preferred_element_type=F32)
            chosen = jnp.where(low_half, summed[:part, 0:128], summed[part:, 0:128])
            divisor = jnp.where(low_half, summed[:part, 128:256], summed[part:, 128:256])
            mixed.append((chosen / divisor).astype(BF))
            yield None
        attended = jnp.concatenate(mixed, axis=1)
        yield (xs[rows, :].astype(F32) + jnp.dot(attended, wout[layer], preferred_element_type=F32)).astype(BF)

    def feed_forward(layer, after):
        middle = after.astype(F32)
        normal = normed(middle, gain_ref[layer, 1:2, :]).astype(BF)
        total = middle
        for j in range(4):
            cols = slice(j * 512, (j + 1) * 512)
            hidden = gelu(jnp.dot(normal, wup[layer, :, cols], preferred_element_type=F32)).astype(BF)
            total = total + jnp.dot(hidden, wdown[layer, cols, :], preferred_element_type=F32)
            yield None
        yield total.astype(BF).reshape(SLOTS, FINE_STEP, D)

    quarter = lax.broadcasted_iota(jnp.int32, (1, 128), 1)

    def pickers(c):
        count = 128 // FINE_STEP
        for j in range(fold):
            shift = (c * fold + j) * FINE_STEP
            for first in range(0, LANES, count):
                chosen = jnp.full((1, 128), table[OWN_BLOCK + first] + shift, jnp.int32)
                for k in range(1, count):
                    lane_key = table[OWN_BLOCK + first + k] + shift - k * FINE_STEP
                    chosen = jnp.where(quarter < k * FINE_STEP, chosen, lane_key)
                at = first * FINE_STEP
                hit = keys_wide[...] == chosen + quarter
                pick_s[c * fold + j, :, at : at + 128] = jnp.where(hit, 1.0, 0.0).astype(BF)

    def receive_and_project(layer, waits, block_of):
        def body(c, carry):
            if layer == 0:
                with scope('pick'):
                    pickers(c)
            for i in range(CHUNKS):
                @pl.when(c == i)
                def _():
                    with scope('wait'):
                        waits(i)
                    for slot in range(SLOTS):
                        for j, piece in enumerate(block_of(i, slot)):
                            at = i * PART + j * SLOTS * FINE_STEP + slot * FINE_STEP
                            xs[at : at + FINE_STEP, :] = piece
            with scope('proj'):
                project(layer, c)
            return carry
        lax.fori_loop(0, CHUNKS, body, 0)


    def wait_x(i):
        gx_all(lanes_a, i, arr_x[i], send_a, recv_a).wait_recv()

    def block_x(i, slot):
        block = arr_x[i][table[FROM_LANE + slot]]
        return [block[j * FINE_STEP : (j + 1) * FINE_STEP, :] for j in range(fold)]

    def wait_1(i):
        for j in range(i * fold, i * fold + fold):
            gy_all(lanes_1, j, arr_1[j], send_1, recv_1).wait_recv()

    def block_1(i, slot):
        return [arr_1[j][table[RECV_LANE + slot]] for j in range(i * fold, i * fold + fold)]

    def forward(i):
        with scope('waitG2'):
            gy_all(lanes_2, i, arr_2[i], send_2, recv_2).wait_recv()
        for k in range(LANES):
            lanes_b[i, k] = arr_2[i][table[HOME_LANE + k]]
        for peer in gx_peers:
            gx_copy(lanes_b.at[i, peer], arr_b.at[i, gx], send_b.at[i], recv_b.at[i], peer).start()
        arr_b[i, gx] = lanes_b[i, gx]

    def compute_and_send(layer, first, lanes, arrived, send, recv, meanwhile):
        def deliver(i):
            for peer in gy_peers:
                pair = pl.ds(peer * 2, 2)
                gy_copy(lanes.at[i, pair], arrived[i].at[pl.ds(gy * 2, 2)], send.at[i], recv.at[i], peer).start()
            for p in range(2):
                arrived[i][gy * 2 + p] = lanes[i, gy * 2 + p]

        def fill(c):
            for lane in range(LANES):
                lanes[c, lane] = y_s[table[first + lane]]

        with scope('att'):
            mid_s[...] = list(attend(layer, 0))[-1]

        def body(c, carry):
            with scope('both'):
                lower = feed_forward(layer, mid_s[...])
                for upper in attend(layer, c + 1):
                    done = next(lower)
                mid_s[...] = upper
                y_s[...] = done
            fill(c)
            for i in range(FINE - 1):
                @pl.when(c == i)
                def _():
                    deliver(i)
                    if meanwhile is not None and i >= 2:
                        meanwhile(i - 2)
            return carry
        lax.fori_loop(0, FINE - 1, body, 0)
        with scope('mlp'):
            y_s[...] = list(feed_forward(layer, mid_s[...]))[-1]
        fill(FINE - 1)
        deliver(FINE - 1)

    loads[1].wait()
    receive_and_project(0, wait_x, block_x)
    for load in loads[2:5]:
        load.wait()
    compute_and_send(0, SEND_SLOT, lanes_1, arr_1, send_1, recv_1, None)
    loads[5].wait()
    receive_and_project(1, wait_1, block_1)
    for load in loads[6:]:
        load.wait()
    compute_and_send(1, BACK_SLOT, lanes_2, arr_2, send_2, recv_2, forward)

    def unpack(*pieces):
        with scope('waitB'):
            for i in pieces:
                gx_all(lanes_b, i, arr_b.at[i], send_b, recv_b).wait_recv()
        for tile in range(4):
            rows = slice(tile * 512, (tile + 1) * 512)
            part = None
            for i in pieces:
                landed = arr_b[i].reshape(LANES * FINE_STEP, D)
                with scope('unp'):
                    piece = jnp.dot(pick_s[i, rows, :], landed, preferred_element_type=F32)
                part = piece if part is None else part + piece
            if pieces[0] == 0:
                out_ref[rows, :] = part.astype(BF)
            else:
                out_ref[rows, :] = out_ref[rows, :] + part.astype(BF)

    forward(FINE - 3)
    forward(FINE - 2)
    unpack(0, 1)
    forward(FINE - 1)
    unpack(2, 3)
    unpack(4, 5)
    unpack(6)
    unpack(7)

    for c in range(CHUNKS):
        gx_all(lanes_a, c, arr_x[c], send_a, recv_a).wait_send()
    for c in range(FINE):
        gy_all(lanes_1, c, arr_1[c], send_1, recv_1).wait_send()
        gy_all(lanes_2, c, arr_2[c], send_2, recv_2).wait_send()
        gx_all(lanes_b, c, arr_b.at[c], send_b, recv_b).wait_send()


def shards(
    features, point_block, block_count, z_dest_dev, z_dest_slot, z_back_owner, z_back_block,
    hil_dest_dev, hil_dest_slot, hil_back_dev, hil_back_slot, norm_gain, w_qkv, w_out, w_up, w_down,
):
    vmem = pl.BlockSpec(memory_space=pltpu.VMEM)
    dma = pltpu.SemaphoreType.DMA
    landing = [pltpu.VMEM((LANES, STEP, D), BF) for _ in range(CHUNKS)]
    landing += [pltpu.VMEM((LANES, FINE_STEP, D), BF) for _ in range(2 * FINE)]
    return pl.pallas_call(
        kernel,
        out_shape=pltpu.VMEM((ROWS, D), BF),
        in_specs=[pl.BlockSpec(memory_space=pltpu.SMEM)] + [pl.BlockSpec(memory_space=pltpu.HBM)] * 12,
        out_specs=vmem,
        scratch_shapes=[
            pltpu.SMEM((1, CAP), jnp.int32),
            pltpu.SMEM((1, SLOTS), jnp.int32),
            pltpu.SMEM((1, SLOTS), jnp.int32),
            pltpu.SMEM((1, SLOTS), jnp.int32),
            pltpu.SMEM((1, SLOTS), jnp.int32),
            pltpu.VMEM((16, 128), jnp.int32),
            pltpu.VMEM((2, 2, D), F32),
            pltpu.SMEM((80,), jnp.int32),
            pltpu.VMEM((ROWS, D), BF),
            pltpu.VMEM((2, D, 3 * D), BF),
            pltpu.VMEM((2, D, D), BF),
            pltpu.VMEM((2, D, FF), BF),
            pltpu.VMEM((2, FF, D), BF),
            pltpu.VMEM((16, 128), jnp.int32),
            pltpu.VMEM((CHUNKS, LANES, STEP, D), BF),
            pltpu.VMEM((ROWS, 128), jnp.int32),
            pltpu.VMEM((FINE, ROWS, LANES * FINE_STEP), BF),
            pltpu.VMEM((SLOTS * BLOCK, D), BF),
            pltpu.VMEM((PAIRS, SLOTS * BLOCK, 128), BF),
            pltpu.VMEM((PAIRS, SLOTS * BLOCK, 128), BF),
            pltpu.VMEM((PAIRS, SLOTS * BLOCK, 256), BF),
            pltpu.VMEM((SLOTS * FINE_STEP, D), BF),
            pltpu.VMEM((SLOTS, FINE_STEP, D), BF),
            pltpu.VMEM((FINE, LANES, FINE_STEP, D), BF),
            pltpu.VMEM((FINE, LANES, FINE_STEP, D), BF),
            pltpu.VMEM((FINE, LANES, FINE_STEP, D), BF),
            pltpu.VMEM((FINE, LANES, FINE_STEP, D), BF),
        ]
        + landing
        + [
            dma((16,)),
            dma((CHUNKS,)), dma((CHUNKS,)), dma((FINE,)), dma((FINE,)),
            dma((FINE,)), dma((FINE,)), dma((FINE,)), dma((FINE,)),
        ],
        compiler_params=pltpu.CompilerParams(
            collective_id=0, has_side_effects=True, vmem_limit_bytes=56 * 1024 * 1024
        ),
    )(
        block_count,
        *[
            pltpu.with_memory_space_constraint(array, pltpu.HBM)
            for array in (
                z_dest_dev, z_back_owner, hil_dest_dev, hil_back_dev, hil_back_slot,
                point_block.reshape(16, 128), norm_gain, features, w_qkv, w_out, w_up, w_down,
            )
        ]
    )


def solution(mesh):
    split = P(("gx", "gy"), None)
    flat = P(("gx", "gy"))
    in_specs = (split, flat, flat) + (split,) * 8 + (P(),) * 5
    return jax.shard_map(shards, mesh=mesh, in_specs=in_specs, out_specs=split, check_vma=False)
```

```python
import contextlib

import jax
import jax.numpy as jnp
from jax import lax
from jax.experimental import pallas as pl
from jax.experimental.pallas import tpu as pltpu
from jax.sharding import PartitionSpec as P

MESH = pl.DeviceIdType.MESH


def scope(name):
    return contextlib.nullcontext()


D = 512
FF = 2048
BLOCK = 128
CAP = 16
SLOTS = 8
ROWS = CAP * BLOCK
CHUNKS = 4
STEP = BLOCK // CHUNKS
PART = SLOTS * STEP
FINE = 8
FINE_STEP = BLOCK // FINE
EARLY = 2
EARLY_KEYS = SLOTS * (BLOCK - STEP)
LANES = 16
PAIRS = 4
EPSILON = 1e-05
BF = jnp.bfloat16
F32 = jnp.float32
SEND_SLOT, RECV_LANE, BACK_SLOT, HOME_LANE, FROM_LANE, OWN_BLOCK = 0, 16, 24, 40, 56, 64
NOWHERE = -1000000

GX_OFFSETS = (
    (0, 1), (1, 0), (0, 3), (3, 0), (1, 1), (3, 3), (1, 3), (3, 1),
    (2, 0), (0, 2), (2, 1), (1, 2), (2, 3), (3, 2), (2, 2),
)
GY_OFFSETS = ((1, 0), (3, 0), (2, 0), (1, 1), (3, 1), (2, 1), (0, 1))


def normed(values_in, gain_row):
    centered = values_in - jnp.mean(values_in, axis=-1, keepdims=True)
    variance = jnp.mean(centered * centered, axis=-1, keepdims=True)
    return centered * lax.rsqrt(variance + EPSILON) * gain_row


def gelu(x):
    inner = x * (0.7978845608028654 + 0.035677408136300125 * (x * x))
    return (0.5 * x) * (1.0 + jnp.tanh(inner))


def row_keys(blocks_of):
    groups = blocks_of.shape[0]
    masks = [jnp.where(blocks_of == b, 1.0, 0.0) for b in range(CAP)]
    stacked = jnp.concatenate(masks, axis=0)
    stacked_low = stacked.astype(BF)
    row = lax.broadcasted_iota(jnp.int32, (128, 128), 0)
    col = lax.broadcasted_iota(jnp.int32, (128, 128), 1)
    before = jnp.where(row < col, 1.0, 0.0).astype(BF)
    within = jnp.dot(stacked_low, before, preferred_element_type=F32)
    totals = jnp.dot(stacked_low, jnp.ones((128, 128), BF), preferred_element_type=F32).astype(BF)
    size = CAP * groups
    high = lax.broadcasted_iota(jnp.int32, (size, size), 0)
    low = lax.broadcasted_iota(jnp.int32, (size, size), 1)
    earlier = jnp.where((high // groups == low // groups) & (low < high), 1.0, 0.0).astype(BF)
    ahead = jnp.dot(earlier, totals, preferred_element_type=F32)
    ranks = within + ahead
    total = jnp.zeros((groups, 128), F32)
    for b in range(CAP):
        part = slice(b * groups, (b + 1) * groups)
        total = total + stacked[part] * (ranks[part] + float(b * BLOCK))
    return total


def own_table(table, counts, z_dest):
    live = counts[0]
    dests = [jnp.where(b < live, z_dest[0, b], -1) for b in range(CAP)]
    for lane in range(LANES):
        chosen = jnp.int32(NOWHERE)
        for b in range(CAP):
            chosen = jnp.where(dests[b] == lane, b * BLOCK, chosen)
        table[OWN_BLOCK + lane] = chosen


def move_tables(table, z_owner, h_dest, h_back, h_slot):
    dest = [h_dest[0, s] for s in range(SLOTS)]
    back = [h_back[0, s] for s in range(SLOTS)]
    slot = [h_slot[0, s] for s in range(SLOTS)]
    owner = [z_owner[0, s] for s in range(SLOTS)]
    send_keys = []
    recv_keys = []
    for s in range(SLOTS):
        key = dest[s] * 2
        for other in range(s):
            key = key + jnp.where(dest[other] == dest[s], 1, 0)
        send_keys.append(key)
        key = back[s] * 2
        for other in range(SLOTS):
            if other != s:
                key = key + jnp.where((back[other] == back[s]) & (slot[other] < slot[s]), 1, 0)
        recv_keys.append(key)
        table[RECV_LANE + s] = key
        table[FROM_LANE + s] = owner[s]
    for lane in range(LANES):
        send = jnp.int32(0)
        back_slot = jnp.int32(0)
        home = jnp.int32(0)
        for s in range(SLOTS):
            send = jnp.where(send_keys[s] == lane, s, send)
            back_slot = jnp.where(recv_keys[s] == lane, s, back_slot)
            home = jnp.where(owner[s] == lane, send_keys[s], home)
        table[SEND_SLOT + lane] = send
        table[BACK_SLOT + lane] = back_slot
        table[HOME_LANE + lane] = home


def kernel(
    counts, z_dest_h, z_owner_h, h_dest_h, h_back_h, h_slot_h, blocks_h, gain_h,
    feat_h, wqkv_h, wout_h, wup_h, wdown_h, out_ref,
    z_dest, z_owner, h_dest, h_back, h_slot, blocks_ref, gain_ref,
    table, feat, wqkv, wout, wup, wdown, keys, lanes_a, keys_wide, pick_s, xs, q_s, k_s, v_s, early_sum, early_max, mid_s, y_s, lanes_1, lanes_2, lanes_b, arr_b,
    *rest,
):
    arr_x, arr_1, arr_2 = rest[:CHUNKS], rest[CHUNKS : CHUNKS + FINE], rest[CHUNKS + FINE : CHUNKS + 2 * FINE]
    local_sem, send_a, recv_a, send_1, recv_1, send_2, recv_2, send_b, recv_b = rest[CHUNKS + 2 * FINE :]
    gx = lax.axis_index("gx")
    gy = lax.axis_index("gy")
    z, y = gx // 4, gx % 4
    x, core = gy // 2, gy % 2
    gx_peers = [((z + dz) % 4) * 4 + (y + dy) % 4 for dz, dy in GX_OFFSETS]
    gy_peers = [((x + dx) % 4) * 2 + (core + dc) % 2 for dx, dc in GY_OFFSETS]

    barrier = pltpu.get_barrier_semaphore()
    for peer in gx_peers:
        pl.semaphore_signal(barrier, inc=1, device_id=(peer, gy), device_id_type=MESH)
    for peer in gy_peers:
        pl.semaphore_signal(barrier, inc=1, device_id=(gx, peer), device_id_type=MESH)

    small = []
    for i, (src, dst) in enumerate(
        (
            (blocks_h, blocks_ref), (z_dest_h, z_dest), (z_owner_h, z_owner),
            (h_dest_h, h_dest), (h_back_h, h_back), (h_slot_h, h_slot), (gain_h, gain_ref),
        )
    ):
        small.append(pltpu.make_async_copy(src, dst, local_sem.at[9 + i]))
    for load in small:
        load.start()
    loads = [pltpu.make_async_copy(feat_h, feat, local_sem.at[0])]
    for layer in range(2):
        for i, (src, dst) in enumerate(((wqkv_h, wqkv), (wout_h, wout), (wup_h, wup), (wdown_h, wdown))):
            loads.append(pltpu.make_async_copy(src.at[layer], dst.at[layer], local_sem.at[1 + layer * 4 + i]))
    for load in loads:
        load.start()

    def gx_copy(src, dst, send, recv, peer):
        return pltpu.make_async_remote_copy(
            src_ref=src, dst_ref=dst, send_sem=send, recv_sem=recv, device_id=(peer, gy), device_id_type=MESH,
        )

    def gy_copy(src, dst, send, recv, peer):
        return pltpu.make_async_remote_copy(
            src_ref=src, dst_ref=dst, send_sem=send, recv_sem=recv, device_id=(gx, peer), device_id_type=MESH,
        )

    def gx_all(lanes, c, arrived, send, recv):
        part = pl.ds(0, LANES - 1)
        return gx_copy(lanes.at[c, part], arrived.at[part], send.at[c], recv.at[c], gx_peers[0])

    def gy_all(lanes, c, arrived, send, recv):
        part = pl.ds(0, LANES - 2)
        return gy_copy(lanes.at[c, part], arrived.at[part], send.at[c], recv.at[c], gy_peers[0])

    for load in small[:2]:
        load.wait()
    own_table(table, counts, z_dest)
    with scope('keys'):
        key_rows = row_keys(blocks_ref[...])
    keys[...] = key_rows.astype(jnp.int32)
    with scope('ldw'):
        loads[0].wait()
    order = gx_peers + [gx]
    for c in range(CHUNKS):
        group = 256 // STEP
        for first in range(0, LANES, group):
            rows_in = lax.broadcasted_iota(jnp.int32, (STEP, 128), 0) + c * STEP
            wanted = jnp.concatenate(
                [rows_in + table[OWN_BLOCK + order[first + k]] for k in range(group)], axis=0
            )
            picker = jnp.concatenate(
                [jnp.where(wanted == keys[g : g + 1, :], 1.0, 0.0).astype(BF) for g in range(16)], axis=1
            )
            with scope('pack'):
                packed = jnp.dot(picker, feat[...], preferred_element_type=F32).astype(BF)
            lanes_a[c, first : first + group] = packed.reshape(group, STEP, D)
            if c == 0 and first == 0:
                with scope('barr'):
                    pl.semaphore_wait(barrier, len(gx_peers) + len(gy_peers))
            for k in range(first, min(first + group, LANES - 1)):
                gx_copy(lanes_a.at[c, k], arr_x[c].at[gx], send_a.at[c], recv_a.at[c], order[k]).start()
        arr_x[c][gx] = lanes_a[c, LANES - 1]

    for load in small[2:]:
        load.wait()
    with scope('mov'):
        move_tables(table, z_owner, h_dest, h_back, h_slot)
    padded = jnp.concatenate([key_rows, jnp.zeros((128 - 16, 128), F32)], axis=0)
    turned = padded.T.astype(jnp.int32)
    for g in range(16):
        keys_wide[g * 128 : (g + 1) * 128, :] = jnp.broadcast_to(turned[:, g : g + 1], (128, 128))


    fold = FINE // CHUNKS

    def project(layer, c):
        rows = pl.ds(c * PART, PART)
        values = xs[rows, :].astype(F32)
        normal = normed(values, gain_ref[layer, 0:1, :]).astype(BF)
        joined = jnp.dot(normal, wqkv[layer], preferred_element_type=F32)
        for pair in range(PAIRS):
            q_s[pair, rows, :] = joined[:, pair * 128 : (pair + 1) * 128].astype(BF) * jnp.asarray(0.125, BF)
            k_s[pair, rows, :] = joined[:, D + pair * 128 : D + (pair + 1) * 128].astype(BF)
            v_s[pair, rows, 0:128] = joined[:, 2 * D + pair * 128 : 2 * D + (pair + 1) * 128].astype(BF)
            v_s[pair, rows, 128:256] = jnp.ones((PART, 128), BF)

    part = SLOTS * FINE_STEP
    low_half = lax.broadcasted_iota(jnp.int32, (part, 128), 1) < 64

    def both_heads(c, pair):
        q_pair = q_s[pair, pl.ds(c * part, part), :]
        zero = jnp.zeros_like(q_pair)
        return jnp.concatenate([jnp.where(low_half, q_pair, zero), jnp.where(low_half, zero, q_pair)], axis=0)

    def against(queries, pair, keys_of):
        return lax.dot_general(
            queries, k_s[pair, keys_of, :], (((1,), (1,)), ((), ())), preferred_element_type=F32
        )

    def attend_early(c):
        keys_of = slice(0, EARLY_KEYS)
        for pair in range(PAIRS):
            scores = against(both_heads(c, pair), pair, keys_of)
            highest = jnp.max(scores, axis=-1, keepdims=True)
            weights = jnp.exp(scores - highest).astype(BF)
            early_sum[c, pair] = jnp.dot(weights, v_s[pair, keys_of, :], preferred_element_type=F32)
            early_max[c, pair] = jnp.broadcast_to(highest, (2 * part, 128))

    def attend(layer, c, early=False):
        keys_of = slice(EARLY_KEYS if early else 0, SLOTS * BLOCK)
        rows = pl.ds(c * part, part)
        mixed = []
        for pair in range(PAIRS):
            scores = against(both_heads(c, pair), pair, keys_of)
            highest = jnp.max(scores, axis=-1, keepdims=True)
            if early:
                before = early_max[c, pair]
                wide = jnp.maximum(jnp.broadcast_to(highest, before.shape), before)
                highest = jnp.concatenate([wide, wide], axis=1)
            weights = jnp.exp(scores - highest).astype(BF)
            summed = jnp.dot(weights, v_s[pair, keys_of, :], preferred_element_type=F32)
            if early:
                kept = jnp.exp(before - wide)
                summed = summed + early_sum[c, pair] * jnp.concatenate([kept, kept], axis=1)
            chosen = jnp.where(low_half, summed[:part, 0:128], summed[part:, 0:128])
            divisor = jnp.where(low_half, summed[:part, 128:256], summed[part:, 128:256])
            mixed.append((chosen / divisor).astype(BF))
            yield None
        attended = jnp.concatenate(mixed, axis=1)
        yield (xs[rows, :].astype(F32) + jnp.dot(attended, wout[layer], preferred_element_type=F32)).astype(BF)

    def feed_forward(layer, after):
        middle = after.astype(F32)
        normal = normed(middle, gain_ref[layer, 1:2, :]).astype(BF)
        total = middle
        for j in range(4):
            cols = slice(j * 512, (j + 1) * 512)
            hidden = gelu(jnp.dot(normal, wup[layer, :, cols], preferred_element_type=F32)).astype(BF)
            total = total + jnp.dot(hidden, wdown[layer, cols, :], preferred_element_type=F32)
            yield None
        yield total.astype(BF).reshape(SLOTS, FINE_STEP, D)

    quarter = lax.broadcasted_iota(jnp.int32, (1, 128), 1)

    def pickers(c):
        count = 128 // FINE_STEP
        for j in range(fold):
            shift = (c * fold + j) * FINE_STEP
            for first in range(0, LANES, count):
                chosen = jnp.full((1, 128), table[OWN_BLOCK + first] + shift, jnp.int32)
                for k in range(1, count):
                    lane_key = table[OWN_BLOCK + first + k] + shift - k * FINE_STEP
                    chosen = jnp.where(quarter < k * FINE_STEP, chosen, lane_key)
                at = first * FINE_STEP
                hit = keys_wide[...] == chosen + quarter
                pick_s[c * fold + j, :, at : at + 128] = jnp.where(hit, 1.0, 0.0).astype(BF)

    def receive_and_project(layer, waits, block_of):
        def body(c, carry):
            if layer == 0:
                with scope('pick'):
                    pickers(c)

            @pl.when(c == CHUNKS - 1)
            def _():
                with scope('early'):
                    for e in range(EARLY):
                        attend_early(e)

            for i in range(CHUNKS):
                @pl.when(c == i)
                def _():
                    with scope('wait'):
                        waits(i)
                    for slot in range(SLOTS):
                        for j, piece in enumerate(block_of(i, slot)):
                            at = i * PART + j * SLOTS * FINE_STEP + slot * FINE_STEP
                            xs[at : at + FINE_STEP, :] = piece
            with scope('proj'):
                project(layer, c)
            return carry
        lax.fori_loop(0, CHUNKS, body, 0)


    def wait_x(i):
        gx_all(lanes_a, i, arr_x[i], send_a, recv_a).wait_recv()

    def block_x(i, slot):
        block = arr_x[i][table[FROM_LANE + slot]]
        return [block[j * FINE_STEP : (j + 1) * FINE_STEP, :] for j in range(fold)]

    def wait_1(i):
        for j in range(i * fold, i * fold + fold):
            gy_all(lanes_1, j, arr_1[j], send_1, recv_1).wait_recv()

    def block_1(i, slot):
        return [arr_1[j][table[RECV_LANE + slot]] for j in range(i * fold, i * fold + fold)]

    def forward(i):
        with scope('waitG2'):
            gy_all(lanes_2, i, arr_2[i], send_2, recv_2).wait_recv()
        for k in range(LANES):
            lanes_b[i, k] = arr_2[i][table[HOME_LANE + k]]
        for peer in gx_peers:
            gx_copy(lanes_b.at[i, peer], arr_b.at[i, gx], send_b.at[i], recv_b.at[i], peer).start()
        arr_b[i, gx] = lanes_b[i, gx]

    def compute_and_send(layer, first, lanes, arrived, send, recv, meanwhile):
        def deliver(i):
            for peer in gy_peers:
                pair = pl.ds(peer * 2, 2)
                gy_copy(lanes.at[i, pair], arrived[i].at[pl.ds(gy * 2, 2)], send.at[i], recv.at[i], peer).start()
            for p in range(2):
                arrived[i][gy * 2 + p] = lanes[i, gy * 2 + p]

        def fill(c):
            for lane in range(LANES):
                lanes[c, lane] = y_s[table[first + lane]]

        def send_off(i):
            deliver(i)
            if meanwhile is not None and i >= 2:
                meanwhile(i - 2)

        def merged(c, early):
            with scope('both'):
                lower = feed_forward(layer, mid_s[...])
                for upper in attend(layer, c + 1, early):
                    done = next(lower)
                mid_s[...] = upper
                y_s[...] = done
            fill(c)

        def body(c, carry):
            merged(c, False)
            for i in range(EARLY - 1, FINE - 1):
                pl.when(c == i)(lambda i=i: send_off(i))
            return carry

        with scope('att'):
            mid_s[...] = list(attend(layer, 0, True))[-1]
        for c in range(EARLY - 1):
            merged(c, True)
            send_off(c)
        lax.fori_loop(EARLY - 1, FINE - 1, body, 0)
        with scope('mlp'):
            y_s[...] = list(feed_forward(layer, mid_s[...]))[-1]
        fill(FINE - 1)
        deliver(FINE - 1)

    loads[1].wait()
    receive_and_project(0, wait_x, block_x)
    for load in loads[2:5]:
        load.wait()
    compute_and_send(0, SEND_SLOT, lanes_1, arr_1, send_1, recv_1, None)
    loads[5].wait()
    receive_and_project(1, wait_1, block_1)
    for load in loads[6:]:
        load.wait()
    compute_and_send(1, BACK_SLOT, lanes_2, arr_2, send_2, recv_2, forward)

    def unpack(*pieces):
        with scope('waitB'):
            for i in pieces:
                gx_all(lanes_b, i, arr_b.at[i], send_b, recv_b).wait_recv()
        for tile in range(4):
            rows = slice(tile * 512, (tile + 1) * 512)
            part = None
            for i in pieces:
                landed = arr_b[i].reshape(LANES * FINE_STEP, D)
                with scope('unp'):
                    piece = jnp.dot(pick_s[i, rows, :], landed, preferred_element_type=F32)
                part = piece if part is None else part + piece
            if pieces[0] == 0:
                out_ref[rows, :] = part.astype(BF)
            else:
                out_ref[rows, :] = out_ref[rows, :] + part.astype(BF)

    forward(FINE - 3)
    forward(FINE - 2)
    unpack(0, 1)
    forward(FINE - 1)
    unpack(2, 3)
    unpack(4, 5)
    unpack(6)
    unpack(7)

    for c in range(CHUNKS):
        gx_all(lanes_a, c, arr_x[c], send_a, recv_a).wait_send()
    for c in range(FINE):
        gy_all(lanes_1, c, arr_1[c], send_1, recv_1).wait_send()
        gy_all(lanes_2, c, arr_2[c], send_2, recv_2).wait_send()
        gx_all(lanes_b, c, arr_b.at[c], send_b, recv_b).wait_send()


def shards(
    features, point_block, block_count, z_dest_dev, z_dest_slot, z_back_owner, z_back_block,
    hil_dest_dev, hil_dest_slot, hil_back_dev, hil_back_slot, norm_gain, w_qkv, w_out, w_up, w_down,
):
    vmem = pl.BlockSpec(memory_space=pltpu.VMEM)
    dma = pltpu.SemaphoreType.DMA
    landing = [pltpu.VMEM((LANES, STEP, D), BF) for _ in range(CHUNKS)]
    landing += [pltpu.VMEM((LANES, FINE_STEP, D), BF) for _ in range(2 * FINE)]
    return pl.pallas_call(
        kernel,
        out_shape=pltpu.VMEM((ROWS, D), BF),
        in_specs=[pl.BlockSpec(memory_space=pltpu.SMEM)] + [pl.BlockSpec(memory_space=pltpu.HBM)] * 12,
        out_specs=vmem,
        scratch_shapes=[
            pltpu.SMEM((1, CAP), jnp.int32),
            pltpu.SMEM((1, SLOTS), jnp.int32),
            pltpu.SMEM((1, SLOTS), jnp.int32),
            pltpu.SMEM((1, SLOTS), jnp.int32),
            pltpu.SMEM((1, SLOTS), jnp.int32),
            pltpu.VMEM((16, 128), jnp.int32),
            pltpu.VMEM((2, 2, D), F32),
            pltpu.SMEM((80,), jnp.int32),
            pltpu.VMEM((ROWS, D), BF),
            pltpu.VMEM((2, D, 3 * D), BF),
            pltpu.VMEM((2, D, D), BF),
            pltpu.VMEM((2, D, FF), BF),
            pltpu.VMEM((2, FF, D), BF),
            pltpu.VMEM((16, 128), jnp.int32),
            pltpu.VMEM((CHUNKS, LANES, STEP, D), BF),
            pltpu.VMEM((ROWS, 128), jnp.int32),
            pltpu.VMEM((FINE, ROWS, LANES * FINE_STEP), BF),
            pltpu.VMEM((SLOTS * BLOCK, D), BF),
            pltpu.VMEM((PAIRS, SLOTS * BLOCK, 128), BF),
            pltpu.VMEM((PAIRS, SLOTS * BLOCK, 128), BF),
            pltpu.VMEM((PAIRS, SLOTS * BLOCK, 256), BF),
            pltpu.VMEM((EARLY, PAIRS, 2 * SLOTS * FINE_STEP, 256), F32),
            pltpu.VMEM((EARLY, PAIRS, 2 * SLOTS * FINE_STEP, 128), F32),
            pltpu.VMEM((SLOTS * FINE_STEP, D), BF),
            pltpu.VMEM((SLOTS, FINE_STEP, D), BF),
            pltpu.VMEM((FINE, LANES, FINE_STEP, D), BF),
            pltpu.VMEM((FINE, LANES, FINE_STEP, D), BF),
            pltpu.VMEM((FINE, LANES, FINE_STEP, D), BF),
            pltpu.VMEM((FINE, LANES, FINE_STEP, D), BF),
        ]
        + landing
        + [
            dma((16,)),
            dma((CHUNKS,)), dma((CHUNKS,)), dma((FINE,)), dma((FINE,)),
            dma((FINE,)), dma((FINE,)), dma((FINE,)), dma((FINE,)),
        ],
        compiler_params=pltpu.CompilerParams(
            collective_id=0, has_side_effects=True, vmem_limit_bytes=56 * 1024 * 1024
        ),
    )(
        block_count,
        *[
            pltpu.with_memory_space_constraint(array, pltpu.HBM)
            for array in (
                z_dest_dev, z_back_owner, hil_dest_dev, hil_back_dev, hil_back_slot,
                point_block.reshape(16, 128), norm_gain, features, w_qkv, w_out, w_up, w_down,
            )
        ]
    )


def solution(mesh):
    split = P(("gx", "gy"), None)
    flat = P(("gx", "gy"))
    in_specs = (split, flat, flat) + (split,) * 8 + (P(),) * 5
    return jax.shard_map(shards, mesh=mesh, in_specs=in_specs, out_specs=split, check_vma=False)
```

```python
import contextlib

import jax
import jax.numpy as jnp
from jax import lax
from jax.experimental import pallas as pl
from jax.experimental.pallas import tpu as pltpu
from jax.sharding import PartitionSpec as P

MESH = pl.DeviceIdType.MESH


def scope(name):
    return contextlib.nullcontext()


D = 512
FF = 2048
BLOCK = 128
CAP = 16
SLOTS = 8
ROWS = CAP * BLOCK
CHUNKS = 4
STEP = BLOCK // CHUNKS
PART = SLOTS * STEP
FINE = 8
FINE_STEP = BLOCK // FINE
EARLY = 3
EARLY_KEYS = SLOTS * (BLOCK - STEP)
LANES = 16
PAIRS = 4
EPSILON = 1e-05
BF = jnp.bfloat16
F32 = jnp.float32
SEND_SLOT, RECV_LANE, BACK_SLOT, HOME_LANE, FROM_LANE, OWN_BLOCK = 0, 16, 24, 40, 56, 64
NOWHERE = -1000000

GX_OFFSETS = (
    (0, 1), (1, 0), (0, 3), (3, 0), (1, 1), (3, 3), (1, 3), (3, 1),
    (2, 0), (0, 2), (2, 1), (1, 2), (2, 3), (3, 2), (2, 2),
)
GY_OFFSETS = ((1, 0), (3, 0), (2, 0), (1, 1), (3, 1), (2, 1), (0, 1))


def normed(values_in, gain_row):
    centered = values_in - jnp.mean(values_in, axis=-1, keepdims=True)
    variance = jnp.mean(centered * centered, axis=-1, keepdims=True)
    return centered * lax.rsqrt(variance + EPSILON) * gain_row


def gelu(x):
    inner = x * (0.7978845608028654 + 0.035677408136300125 * (x * x))
    return (0.5 * x) * (1.0 + jnp.tanh(inner))


def row_keys(blocks_of):
    groups = blocks_of.shape[0]
    masks = [jnp.where(blocks_of == b, 1.0, 0.0) for b in range(CAP)]
    stacked = jnp.concatenate(masks, axis=0)
    stacked_low = stacked.astype(BF)
    row = lax.broadcasted_iota(jnp.int32, (128, 128), 0)
    col = lax.broadcasted_iota(jnp.int32, (128, 128), 1)
    before = jnp.where(row < col, 1.0, 0.0).astype(BF)
    within = jnp.dot(stacked_low, before, preferred_element_type=F32)
    totals = jnp.dot(stacked_low, jnp.ones((128, 128), BF), preferred_element_type=F32).astype(BF)
    size = CAP * groups
    high = lax.broadcasted_iota(jnp.int32, (size, size), 0)
    low = lax.broadcasted_iota(jnp.int32, (size, size), 1)
    earlier = jnp.where((high // groups == low // groups) & (low < high), 1.0, 0.0).astype(BF)
    ahead = jnp.dot(earlier, totals, preferred_element_type=F32)
    ranks = within + ahead
    total = jnp.zeros((groups, 128), F32)
    for b in range(CAP):
        part = slice(b * groups, (b + 1) * groups)
        total = total + stacked[part] * (ranks[part] + float(b * BLOCK))
    return total


def own_table(table, counts, z_dest):
    live = counts[0]
    dests = [jnp.where(b < live, z_dest[0, b], -1) for b in range(CAP)]
    for lane in range(LANES):
        chosen = jnp.int32(NOWHERE)
        for b in range(CAP):
            chosen = jnp.where(dests[b] == lane, b * BLOCK, chosen)
        table[OWN_BLOCK + lane] = chosen


def move_tables(table, z_owner, h_dest, h_back, h_slot):
    dest = [h_dest[0, s] for s in range(SLOTS)]
    back = [h_back[0, s] for s in range(SLOTS)]
    slot = [h_slot[0, s] for s in range(SLOTS)]
    owner = [z_owner[0, s] for s in range(SLOTS)]
    send_keys = []
    recv_keys = []
    for s in range(SLOTS):
        key = dest[s] * 2
        for other in range(s):
            key = key + jnp.where(dest[other] == dest[s], 1, 0)
        send_keys.append(key)
        key = back[s] * 2
        for other in range(SLOTS):
            if other != s:
                key = key + jnp.where((back[other] == back[s]) & (slot[other] < slot[s]), 1, 0)
        recv_keys.append(key)
        table[RECV_LANE + s] = key
        table[FROM_LANE + s] = owner[s]
    for lane in range(LANES):
        send = jnp.int32(0)
        back_slot = jnp.int32(0)
        home = jnp.int32(0)
        for s in range(SLOTS):
            send = jnp.where(send_keys[s] == lane, s, send)
            back_slot = jnp.where(recv_keys[s] == lane, s, back_slot)
            home = jnp.where(owner[s] == lane, send_keys[s], home)
        table[SEND_SLOT + lane] = send
        table[BACK_SLOT + lane] = back_slot
        table[HOME_LANE + lane] = home


def kernel(
    counts, z_dest_h, z_owner_h, h_dest_h, h_back_h, h_slot_h, blocks_h, gain_h,
    feat_h, wqkv_h, wout_h, wup_h, wdown_h, out_ref,
    z_dest, z_owner, h_dest, h_back, h_slot, blocks_ref, gain_ref,
    table, feat, wqkv, wout, wup, wdown, keys, lanes_a, keys_wide, pick_s, xs, q_s, k_s, v_s, early_sum, early_max, mid_s, y_s, lanes_1, lanes_2, lanes_b, arr_b,
    *rest,
):
    arr_x, arr_1, arr_2 = rest[:CHUNKS], rest[CHUNKS : CHUNKS + FINE], rest[CHUNKS + FINE : CHUNKS + 2 * FINE]
    local_sem, send_a, recv_a, send_1, recv_1, send_2, recv_2, send_b, recv_b = rest[CHUNKS + 2 * FINE :]
    gx = lax.axis_index("gx")
    gy = lax.axis_index("gy")
    z, y = gx // 4, gx % 4
    x, core = gy // 2, gy % 2
    gx_peers = [((z + dz) % 4) * 4 + (y + dy) % 4 for dz, dy in GX_OFFSETS]
    gy_peers = [((x + dx) % 4) * 2 + (core + dc) % 2 for dx, dc in GY_OFFSETS]

    barrier = pltpu.get_barrier_semaphore()
    for peer in gx_peers:
        pl.semaphore_signal(barrier, inc=1, device_id=(peer, gy), device_id_type=MESH)
    for peer in gy_peers:
        pl.semaphore_signal(barrier, inc=1, device_id=(gx, peer), device_id_type=MESH)

    small = []
    for i, (src, dst) in enumerate(
        (
            (blocks_h, blocks_ref), (z_dest_h, z_dest), (z_owner_h, z_owner),
            (h_dest_h, h_dest), (h_back_h, h_back), (h_slot_h, h_slot), (gain_h, gain_ref),
        )
    ):
        small.append(pltpu.make_async_copy(src, dst, local_sem.at[9 + i]))
    for load in small:
        load.start()
    loads = [pltpu.make_async_copy(feat_h, feat, local_sem.at[0])]
    for layer in range(2):
        for i, (src, dst) in enumerate(((wqkv_h, wqkv), (wout_h, wout), (wup_h, wup), (wdown_h, wdown))):
            loads.append(pltpu.make_async_copy(src.at[layer], dst.at[layer], local_sem.at[1 + layer * 4 + i]))
    for load in loads:
        load.start()

    def gx_copy(src, dst, send, recv, peer):
        return pltpu.make_async_remote_copy(
            src_ref=src, dst_ref=dst, send_sem=send, recv_sem=recv, device_id=(peer, gy), device_id_type=MESH,
        )

    def gy_copy(src, dst, send, recv, peer):
        return pltpu.make_async_remote_copy(
            src_ref=src, dst_ref=dst, send_sem=send, recv_sem=recv, device_id=(gx, peer), device_id_type=MESH,
        )

    def gx_all(lanes, c, arrived, send, recv):
        part = pl.ds(0, LANES - 1)
        return gx_copy(lanes.at[c, part], arrived.at[part], send.at[c], recv.at[c], gx_peers[0])

    def gy_all(lanes, c, arrived, send, recv):
        part = pl.ds(0, LANES - 2)
        return gy_copy(lanes.at[c, part], arrived.at[part], send.at[c], recv.at[c], gy_peers[0])

    for load in small[:2]:
        load.wait()
    own_table(table, counts, z_dest)
    with scope('keys'):
        key_rows = row_keys(blocks_ref[...])
    keys[...] = key_rows.astype(jnp.int32)
    with scope('ldw'):
        loads[0].wait()
    order = gx_peers + [gx]
    for c in range(CHUNKS):
        group = 256 // STEP
        for first in range(0, LANES, group):
            rows_in = lax.broadcasted_iota(jnp.int32, (STEP, 128), 0) + c * STEP
            wanted = jnp.concatenate(
                [rows_in + table[OWN_BLOCK + order[first + k]] for k in range(group)], axis=0
            )
            picker = jnp.concatenate(
                [jnp.where(wanted == keys[g : g + 1, :], 1.0, 0.0).astype(BF) for g in range(16)], axis=1
            )
            with scope('pack'):
                packed = jnp.dot(picker, feat[...], preferred_element_type=F32).astype(BF)
            lanes_a[c, first : first + group] = packed.reshape(group, STEP, D)
            if c == 0 and first == 0:
                with scope('barr'):
                    pl.semaphore_wait(barrier, len(gx_peers) + len(gy_peers))
            for k in range(first, min(first + group, LANES - 1)):
                gx_copy(lanes_a.at[c, k], arr_x[c].at[gx], send_a.at[c], recv_a.at[c], order[k]).start()
        arr_x[c][gx] = lanes_a[c, LANES - 1]

    for load in small[2:]:
        load.wait()
    with scope('mov'):
        move_tables(table, z_owner, h_dest, h_back, h_slot)
    padded = jnp.concatenate([key_rows, jnp.zeros((128 - 16, 128), F32)], axis=0)
    turned = padded.T.astype(jnp.int32)
    for g in range(16):
        keys_wide[g * 128 : (g + 1) * 128, :] = jnp.broadcast_to(turned[:, g : g + 1], (128, 128))


    fold = FINE // CHUNKS

    def project(layer, c):
        rows = pl.ds(c * PART, PART)
        values = xs[rows, :].astype(F32)
        normal = normed(values, gain_ref[layer, 0:1, :]).astype(BF)
        joined = jnp.dot(normal, wqkv[layer], preferred_element_type=F32)
        for pair in range(PAIRS):
            q_s[pair, rows, :] = joined[:, pair * 128 : (pair + 1) * 128].astype(BF) * jnp.asarray(0.125, BF)
            k_s[pair, rows, :] = joined[:, D + pair * 128 : D + (pair + 1) * 128].astype(BF)
            v_s[pair, rows, 0:128] = joined[:, 2 * D + pair * 128 : 2 * D + (pair + 1) * 128].astype(BF)
            v_s[pair, rows, 128:256] = jnp.ones((PART, 128), BF)

    part = SLOTS * FINE_STEP
    low_half = lax.broadcasted_iota(jnp.int32, (part, 128), 1) < 64

    def both_heads(c, pair):
        q_pair = q_s[pair, pl.ds(c * part, part), :]
        zero = jnp.zeros_like(q_pair)
        return jnp.concatenate([jnp.where(low_half, q_pair, zero), jnp.where(low_half, zero, q_pair)], axis=0)

    def against(queries, pair, keys_of):
        return lax.dot_general(
            queries, k_s[pair, keys_of, :], (((1,), (1,)), ((), ())), preferred_element_type=F32
        )

    def attend_early(c):
        keys_of = slice(0, EARLY_KEYS)
        for pair in range(PAIRS):
            scores = against(both_heads(c, pair), pair, keys_of)
            highest = jnp.max(scores, axis=-1, keepdims=True)
            weights = jnp.exp(scores - highest).astype(BF)
            early_sum[c, pair] = jnp.dot(weights, v_s[pair, keys_of, :], preferred_element_type=F32)
            early_max[c, pair] = jnp.broadcast_to(highest, (2 * part, 128))

    def attend(layer, c, early=False):
        keys_of = slice(EARLY_KEYS if early else 0, SLOTS * BLOCK)
        rows = pl.ds(c * part, part)
        mixed = []
        for pair in range(PAIRS):
            scores = against(both_heads(c, pair), pair, keys_of)
            highest = jnp.max(scores, axis=-1, keepdims=True)
            if early:
                before = early_max[c, pair]
                wide = jnp.maximum(jnp.broadcast_to(highest, before.shape), before)
                highest = jnp.concatenate([wide, wide], axis=1)
            weights = jnp.exp(scores - highest).astype(BF)
            summed = jnp.dot(weights, v_s[pair, keys_of, :], preferred_element_type=F32)
            if early:
                kept = jnp.exp(before - wide)
                summed = summed + early_sum[c, pair] * jnp.concatenate([kept, kept], axis=1)
            chosen = jnp.where(low_half, summed[:part, 0:128], summed[part:, 0:128])
            divisor = jnp.where(low_half, summed[:part, 128:256], summed[part:, 128:256])
            mixed.append((chosen / divisor).astype(BF))
            yield None
        attended = jnp.concatenate(mixed, axis=1)
        yield (xs[rows, :].astype(F32) + jnp.dot(attended, wout[layer], preferred_element_type=F32)).astype(BF)

    def feed_forward(layer, after):
        middle = after.astype(F32)
        normal = normed(middle, gain_ref[layer, 1:2, :]).astype(BF)
        total = middle
        for j in range(4):
            cols = slice(j * 512, (j + 1) * 512)
            hidden = gelu(jnp.dot(normal, wup[layer, :, cols], preferred_element_type=F32)).astype(BF)
            total = total + jnp.dot(hidden, wdown[layer, cols, :], preferred_element_type=F32)
            yield None
        yield total.astype(BF).reshape(SLOTS, FINE_STEP, D)

    quarter = lax.broadcasted_iota(jnp.int32, (1, 128), 1)

    def pickers(c):
        count = 128 // FINE_STEP
        for j in range(fold):
            shift = (c * fold + j) * FINE_STEP
            for first in range(0, LANES, count):
                chosen = jnp.full((1, 128), table[OWN_BLOCK + first] + shift, jnp.int32)
                for k in range(1, count):
                    lane_key = table[OWN_BLOCK + first + k] + shift - k * FINE_STEP
                    chosen = jnp.where(quarter < k * FINE_STEP, chosen, lane_key)
                at = first * FINE_STEP
                hit = keys_wide[...] == chosen + quarter
                pick_s[c * fold + j, :, at : at + 128] = jnp.where(hit, 1.0, 0.0).astype(BF)

    def receive_and_project(layer, waits, block_of):
        def body(c, carry):
            if layer == 0:
                with scope('pick'):
                    pickers(c)

            @pl.when(c == CHUNKS - 1)
            def _():
                with scope('early'):
                    for e in range(EARLY):
                        attend_early(e)

            for i in range(CHUNKS):
                @pl.when(c == i)
                def _():
                    with scope('wait'):
                        waits(i)
                    for slot in range(SLOTS):
                        for j, piece in enumerate(block_of(i, slot)):
                            at = i * PART + j * SLOTS * FINE_STEP + slot * FINE_STEP
                            xs[at : at + FINE_STEP, :] = piece
            with scope('proj'):
                project(layer, c)
            return carry
        lax.fori_loop(0, CHUNKS, body, 0)


    def wait_x(i):
        gx_all(lanes_a, i, arr_x[i], send_a, recv_a).wait_recv()

    def block_x(i, slot):
        block = arr_x[i][table[FROM_LANE + slot]]
        return [block[j * FINE_STEP : (j + 1) * FINE_STEP, :] for j in range(fold)]

    def wait_1(i):
        for j in range(i * fold, i * fold + fold):
            gy_all(lanes_1, j, arr_1[j], send_1, recv_1).wait_recv()

    def block_1(i, slot):
        return [arr_1[j][table[RECV_LANE + slot]] for j in range(i * fold, i * fold + fold)]

    def forward(i):
        with scope('waitG2'):
            gy_all(lanes_2, i, arr_2[i], send_2, recv_2).wait_recv()
        for k in range(LANES):
            lanes_b[i, k] = arr_2[i][table[HOME_LANE + k]]
        for peer in gx_peers:
            gx_copy(lanes_b.at[i, peer], arr_b.at[i, gx], send_b.at[i], recv_b.at[i], peer).start()
        arr_b[i, gx] = lanes_b[i, gx]

    def compute_and_send(layer, first, lanes, arrived, send, recv, meanwhile):
        def deliver(i):
            for peer in gy_peers:
                pair = pl.ds(peer * 2, 2)
                gy_copy(lanes.at[i, pair], arrived[i].at[pl.ds(gy * 2, 2)], send.at[i], recv.at[i], peer).start()
            for p in range(2):
                arrived[i][gy * 2 + p] = lanes[i, gy * 2 + p]

        def fill(c):
            for lane in range(LANES):
                lanes[c, lane] = y_s[table[first + lane]]

        def send_off(i):
            deliver(i)
            if meanwhile is not None and i >= 2:
                meanwhile(i - 2)

        def merged(c):
            with scope('both'):
                lower = feed_forward(layer, mid_s[...])
                for upper in attend(layer, c + 1):
                    done = next(lower)
                mid_s[...] = upper
                y_s[...] = done
            fill(c)

        def body(c, carry):
            merged(c)
            for i in range(EARLY - 1, FINE - 1):
                pl.when(c == i)(lambda i=i: send_off(i))
            return carry

        for c in range(EARLY - 1):
            with scope('att'):
                mid_s[...] = list(attend(layer, c, True))[-1]
                y_s[...] = list(feed_forward(layer, mid_s[...]))[-1]
            fill(c)
            send_off(c)
        with scope('att'):
            mid_s[...] = list(attend(layer, EARLY - 1, True))[-1]
        lax.fori_loop(EARLY - 1, FINE - 1, body, 0)
        with scope('mlp'):
            y_s[...] = list(feed_forward(layer, mid_s[...]))[-1]
        fill(FINE - 1)
        deliver(FINE - 1)

    loads[1].wait()
    receive_and_project(0, wait_x, block_x)
    for load in loads[2:5]:
        load.wait()
    compute_and_send(0, SEND_SLOT, lanes_1, arr_1, send_1, recv_1, None)
    loads[5].wait()
    receive_and_project(1, wait_1, block_1)
    for load in loads[6:]:
        load.wait()
    compute_and_send(1, BACK_SLOT, lanes_2, arr_2, send_2, recv_2, forward)

    def unpack(*pieces):
        with scope('waitB'):
            for i in pieces:
                gx_all(lanes_b, i, arr_b.at[i], send_b, recv_b).wait_recv()
        for tile in range(4):
            rows = slice(tile * 512, (tile + 1) * 512)
            part = None
            for i in pieces:
                landed = arr_b[i].reshape(LANES * FINE_STEP, D)
                with scope('unp'):
                    piece = jnp.dot(pick_s[i, rows, :], landed, preferred_element_type=F32)
                part = piece if part is None else part + piece
            if pieces[0] == 0:
                out_ref[rows, :] = part.astype(BF)
            else:
                out_ref[rows, :] = out_ref[rows, :] + part.astype(BF)

    forward(FINE - 3)
    forward(FINE - 2)
    unpack(0, 1)
    forward(FINE - 1)
    unpack(2, 3)
    unpack(4, 5)
    unpack(6)
    unpack(7)

    for c in range(CHUNKS):
        gx_all(lanes_a, c, arr_x[c], send_a, recv_a).wait_send()
    for c in range(FINE):
        gy_all(lanes_1, c, arr_1[c], send_1, recv_1).wait_send()
        gy_all(lanes_2, c, arr_2[c], send_2, recv_2).wait_send()
        gx_all(lanes_b, c, arr_b.at[c], send_b, recv_b).wait_send()


def shards(
    features, point_block, block_count, z_dest_dev, z_dest_slot, z_back_owner, z_back_block,
    hil_dest_dev, hil_dest_slot, hil_back_dev, hil_back_slot, norm_gain, w_qkv, w_out, w_up, w_down,
):
    vmem = pl.BlockSpec(memory_space=pltpu.VMEM)
    dma = pltpu.SemaphoreType.DMA
    landing = [pltpu.VMEM((LANES, STEP, D), BF) for _ in range(CHUNKS)]
    landing += [pltpu.VMEM((LANES, FINE_STEP, D), BF) for _ in range(2 * FINE)]
    return pl.pallas_call(
        kernel,
        out_shape=pltpu.VMEM((ROWS, D), BF),
        in_specs=[pl.BlockSpec(memory_space=pltpu.SMEM)] + [pl.BlockSpec(memory_space=pltpu.HBM)] * 12,
        out_specs=vmem,
        scratch_shapes=[
            pltpu.SMEM((1, CAP), jnp.int32),
            pltpu.SMEM((1, SLOTS), jnp.int32),
            pltpu.SMEM((1, SLOTS), jnp.int32),
            pltpu.SMEM((1, SLOTS), jnp.int32),
            pltpu.SMEM((1, SLOTS), jnp.int32),
            pltpu.VMEM((16, 128), jnp.int32),
            pltpu.VMEM((2, 2, D), F32),
            pltpu.SMEM((80,), jnp.int32),
            pltpu.VMEM((ROWS, D), BF),
            pltpu.VMEM((2, D, 3 * D), BF),
            pltpu.VMEM((2, D, D), BF),
            pltpu.VMEM((2, D, FF), BF),
            pltpu.VMEM((2, FF, D), BF),
            pltpu.VMEM((16, 128), jnp.int32),
            pltpu.VMEM((CHUNKS, LANES, STEP, D), BF),
            pltpu.VMEM((ROWS, 128), jnp.int32),
            pltpu.VMEM((FINE, ROWS, LANES * FINE_STEP), BF),
            pltpu.VMEM((SLOTS * BLOCK, D), BF),
            pltpu.VMEM((PAIRS, SLOTS * BLOCK, 128), BF),
            pltpu.VMEM((PAIRS, SLOTS * BLOCK, 128), BF),
            pltpu.VMEM((PAIRS, SLOTS * BLOCK, 256), BF),
            pltpu.VMEM((EARLY, PAIRS, 2 * SLOTS * FINE_STEP, 256), F32),
            pltpu.VMEM((EARLY, PAIRS, 2 * SLOTS * FINE_STEP, 128), F32),
            pltpu.VMEM((SLOTS * FINE_STEP, D), BF),
            pltpu.VMEM((SLOTS, FINE_STEP, D), BF),
            pltpu.VMEM((FINE, LANES, FINE_STEP, D), BF),
            pltpu.VMEM((FINE, LANES, FINE_STEP, D), BF),
            pltpu.VMEM((FINE, LANES, FINE_STEP, D), BF),
            pltpu.VMEM((FINE, LANES, FINE_STEP, D), BF),
        ]
        + landing
        + [
            dma((16,)),
            dma((CHUNKS,)), dma((CHUNKS,)), dma((FINE,)), dma((FINE,)),
            dma((FINE,)), dma((FINE,)), dma((FINE,)), dma((FINE,)),
        ],
        compiler_params=pltpu.CompilerParams(
            collective_id=0, has_side_effects=True, vmem_limit_bytes=56 * 1024 * 1024
        ),
    )(
        block_count,
        *[
            pltpu.with_memory_space_constraint(array, pltpu.HBM)
            for array in (
                z_dest_dev, z_back_owner, hil_dest_dev, hil_back_dev, hil_back_slot,
                point_block.reshape(16, 128), norm_gain, features, w_qkv, w_out, w_up, w_down,
            )
        ]
    )


def solution(mesh):
    split = P(("gx", "gy"), None)
    flat = P(("gx", "gy"))
    in_specs = (split, flat, flat) + (split,) * 8 + (P(),) * 5
    return jax.shard_map(shards, mesh=mesh, in_specs=in_specs, out_specs=split, check_vma=False)
```
